32 devices in a mesh: seq: 16 (over z, x, core), head: 2 (over y).
Axes of the slice: x: 2, y: 2, z: 4, core: 2. Of those that a mesh axis runs over, the one named last changes fastest.
Arguments:
- queries: bfloat16 [4096, 4096], P('seq', 'head'), may hold values from -8 to 8
- keys: bfloat16 [4096, 4096], P('seq', 'head'), may hold values from -8 to 8
- values: bfloat16 [4096, 4096], P('seq', 'head'), may hold values from -6 to 6
- features: float32 [32, 128, 256], P('head'), may hold values from -6 to 6
- output_proj_weight: bfloat16 [4096, 4096], P('head', 'seq'), may hold values from -0.125 to 0.125
Outputs:
- mixed: bfloat16 [4096, 4096], P('seq', 'head')
The draws below stay inside these ranges and needn't reach their ends.
All inputs are finite; a program needn't handle non-finite values.
Results may differ from the reference program's by a relative error of at most 0.005.
Values may be sent and summed in bfloat16 or wider, within the bound.
A program may use at most 192 MiB of HBM per device.

```python
import math
import jax
import jax.numpy as jnp
from jax import lax

D = 4096
HEADS = 32
DH = 128
M = 256
TOKENS = 4096


def spiked(values, own_key, source, target, blocks, factor):
    owner, partner = [(jnp.arange(values.shape[axis_at]) // (values.shape[axis_at] // blocks)).reshape([-1 if axis == axis_at else 1 for axis in range(values.ndim)]) for axis_at in (source, target)]
    chosen = jax.random.permutation(own_key, blocks)[partner]
    strong = (owner == chosen) | (owner == (partner + blocks // 2) % blocks)
    return jnp.where(strong, factor * values, values)


def levels(stream_key, extent, split, low, high):
    loudness = 1.0
    for position, shards_of in split:
        draws = jax.random.uniform(jax.random.fold_in(jax.random.fold_in(stream_key, 6), position), (shards_of,), jnp.float32, low / len(split), high / len(split))
        loudness = loudness * jnp.repeat(jnp.exp(draws), extent[position] // shards_of).reshape((-1,) + (1,) * (len(extent) - 1 - position))
    return loudness


def noise(own_key, extent, spread, most, split=(), kind=jnp.bfloat16):
    level = levels(own_key, extent, split, -0.22, 0.18) if split else 1.0
    values = jax.random.normal(own_key, extent, jnp.float32) * spread * level
    return jnp.minimum(jnp.maximum(values, -most), most).astype(kind)


def heavy_noise(own_key, dims, scale, reach, split, heavy, held_as=jnp.bfloat16):
    values = scale * jax.random.normal(own_key, dims, jnp.float32)
    if split:
        values = values * levels(own_key, dims, split, -0.22, 0.18)
    return jnp.clip(spiked(values, jax.random.fold_in(own_key, 3), *heavy), -reach, reach).astype(held_as)


def setup_inputs(seed: int = 0) -> dict:
    splits = jax.random.split(jax.random.key(seed), 6)
    return {
        "queries": noise(splits[0], (TOKENS, HEADS * DH), 1.25, 8.0, ((0, 16), (1, 2))),
        "keys": noise(splits[1], (TOKENS, HEADS * DH), 1.25, 8.0, ((0, 16), (1, 2))),
        "values": noise(splits[2], (TOKENS, HEADS * DH), 1.0, 6.0, ((0, 16), (1, 2))),
        "features": noise(splits[3], (HEADS, DH, M), 1.0, 6.0, ((0, 2),), jnp.float32),
        "output_proj_weight": heavy_noise(splits[4], (HEADS * DH, D), (HEADS * DH) ** -0.5, 0.125, ((0, 2), (1, 16)), (0, 1, 16, 2.0)),
    }


def feature_map(x, direction):
    x = x * DH ** (-0.25)
    proj = jnp.dot(x, direction, precision=lax.Precision.HIGHEST)
    return jnp.exp(proj - 0.5 * lax.optimization_barrier(jnp.sum(x * x, axis=-1, keepdims=True))) / math.sqrt(M)

def head_attend(inputs):
    query, key, value, direction = inputs
    block = math.gcd(TOKENS, 512)
    count = TOKENS // block
    query = query.reshape(count, block, DH)
    key = key.reshape(count, block, DH)
    value = value.reshape(count, block, DH)
    lower = jnp.tril(jnp.ones((block, block), jnp.float32))

    def step(carry, piece):
        state, total = carry
        q_block, k_block, v_block = piece
        query_random_feats = feature_map(q_block, direction)
        key_random_feats = feature_map(k_block, direction)
        causal_scores = jnp.dot(query_random_feats, key_random_feats.T, precision=lax.Precision.HIGHEST) * lower
        numer = jnp.dot(causal_scores, v_block, precision=lax.Precision.HIGHEST) + jnp.dot(query_random_feats, state, precision=lax.Precision.HIGHEST)
        denom = lax.optimization_barrier(jnp.sum(causal_scores, axis=1)) + jnp.dot(query_random_feats, total, precision=lax.Precision.HIGHEST)
        state = state + jnp.dot(key_random_feats.T, v_block, precision=lax.Precision.HIGHEST)
        total = total + lax.optimization_barrier(jnp.sum(key_random_feats, axis=0))
        return ((state, total), numer / denom[:, None])
    init = (jnp.zeros((M, DH), jnp.float32), jnp.zeros((M,), jnp.float32))
    _, final_output = lax.scan(step, init, (query, key, value))
    return final_output.reshape(TOKENS, DH)

def reference(queries, keys, values, features, output_proj_weight):

    def split_heads(arr):
        return arr.astype(jnp.float32).reshape(TOKENS, HEADS, DH).transpose(1, 0, 2)
    final_output = lax.map(head_attend, (split_heads(queries), split_heads(keys), split_heads(values), features))
    attended = final_output.transpose(1, 0, 2).reshape(TOKENS, HEADS * DH).astype(jnp.bfloat16)
    return jnp.dot(attended, output_proj_weight, preferred_element_type=jnp.float32).astype(jnp.bfloat16)
```

```python
import math

import jax
import jax.numpy as jnp
from jax import lax
from jax.experimental import pallas as pl
from jax.experimental.pallas import tpu as pltpu
from jax.sharding import PartitionSpec as P

DH = 128
M = 256
HIGH = lax.Precision.HIGHEST


def feature_map(x, direction):
    x = x * DH ** (-0.25)
    proj = jnp.einsum("htd,hdm->htm", x, direction, precision=HIGH)
    return jnp.exp(proj - 0.5 * jnp.sum(x * x, axis=-1, keepdims=True)) / math.sqrt(M)


def plain(queries, keys, values, features, output_proj_weight):
    tok_rows = queries.shape[0]
    local_heads = features.shape[0]
    devices, here = lax.axis_size("seq"), lax.axis_index("seq")
    halves, half = lax.axis_size("head"), lax.axis_index("head")

    def split_heads(arr):
        return arr.astype(jnp.float32).reshape(tok_rows, local_heads, DH).transpose(1, 0, 2)

    kf = feature_map(split_heads(keys), features)
    v = split_heads(values)
    v = jnp.concatenate([v, jnp.ones((local_heads, tok_rows, 8), jnp.float32)], axis=2)
    state = jnp.einsum("htp,htk->hpk", v, kf, precision=HIGH)
    states = lax.all_gather(state.astype(jnp.bfloat16), "seq")
    state, weight = lax.optimization_barrier((state, output_proj_weight))
    whole = lax.all_gather(weight, "seq", axis=1, tiled=True)
    qf = feature_map(split_heads(queries), features)
    lower = jnp.tril(jnp.ones((tok_rows, tok_rows), jnp.float32))
    scores = jnp.einsum("htm,hsm->hts", qf, kf, precision=HIGH) * lower
    both = jnp.einsum("hts,hsd->htd", scores, v, precision=HIGH)
    earlier = (jnp.arange(devices) < here)[:, None, None, None]
    prior = jnp.sum(jnp.where(earlier, states.astype(jnp.float32), 0.0), axis=0)
    both = both + jnp.einsum("htk,hpk->htp", qf, prior, precision=HIGH)
    attended = both[:, :, :DH] / both[:, :, DH : DH + 1]
    attended = attended.transpose(1, 0, 2).reshape(tok_rows, local_heads * DH).astype(jnp.bfloat16)
    partial = jnp.dot(attended, whole, preferred_element_type=jnp.float32)
    width = partial.shape[1] // halves
    total = lax.dynamic_slice_in_dim(partial, half * width, width, 1)
    for shift in range(1, halves):
        theirs = lax.rem(half + shift, halves)
        piece = lax.dynamic_slice_in_dim(partial, theirs * width, width, 1).astype(jnp.bfloat16)
        got = lax.ppermute(piece, "head", [(i, (i + shift) % halves) for i in range(halves)])
        total = total + got.astype(jnp.float32)
    return total.astype(jnp.bfloat16)


PLANE, DEPTH = 4, 4
PER = 2
GROUPS = 4
TAIL = 16
LOG2E = math.log2(math.e)


def kernel_body(q_hbm, k_hbm, v_hbm, f_hbm, w_hbm, out_ref, q_ref, k_ref, v_ref, f_ref, wbuf, fhl,
                kf, qf, vt, both, own32, sibst, sbsend, xsend, xrecv, below, back, xpsend, xprior,
                prior, sbp, attb, acc, psend, precv, osend, obuf,
                in_sem, w_load, w_send, w_recv, sb_send, sb_recv, x_send, x_recv, z_send, z_recv,
                xp_send, xp_recv, sp_send, sp_recv, at_send, at_recv, p_send, p_recv,
                o_send, o_recv):
    f32, bf16 = jnp.float32, jnp.bfloat16
    tok = q_ref.shape[0]
    htok = tok // 2
    heads = f_ref.shape[0]
    depth = w_hbm.shape[0]
    hdepth = depth // 2
    me, y = lax.axis_index("seq"), lax.axis_index("head")
    z, x, c = me // PLANE, (me // 2) % 2, me % 2
    sib, xn, up, down = me + 1 - 2 * c, me + 2 - 4 * x, me + PLANE, me - PLANE
    pz = me + PLANE - 2 * PLANE * (z % 2)
    pzsib = pz + 1 - 2 * c
    far = me + 2 * PLANE - 4 * PLANE * (z // 2)
    has_up, has_down = z < DEPTH - 1, z > 0
    low = z < 2

    loads = [pltpu.make_async_copy(a, b, in_sem.at[i]) for i, (a, b) in enumerate(
        ((k_hbm, k_ref), (f_hbm, f_ref), (v_hbm, v_ref), (q_hbm, q_ref)))]
    for one in loads:
        one.start()
    barrier = pltpu.get_barrier_semaphore()

    def greet(device):
        pl.semaphore_signal(barrier, inc=1, device_id=device, device_id_type=pl.DeviceIdType.MESH)

    for device in ((sib, y), (xn, y), (me, 1 - y), (far, y), (pzsib, y)):
        greet(device)

    @pl.when(has_up)
    def _():
        greet((up, y))

    @pl.when(has_down)
    def _():
        greet((down, y))

    pl.semaphore_wait(barrier, 5 + has_up.astype(jnp.int32) + has_down.astype(jnp.int32))

    def remote(src, dst, ssem, rsem, device):
        return pltpu.make_async_remote_copy(
            src_ref=src, dst_ref=dst, send_sem=ssem, recv_sem=rsem, device_id=device,
            device_id_type=pl.DeviceIdType.MESH)

    started = []

    def go(cond, copy):
        if cond is None:
            copy.start()
        else:
            pl.when(cond)(copy.start)
        started.append((cond, copy))

    def place(slot, q):
        return wbuf.at[2 * slot + q // 2, pl.ds((q % 2) * hdepth, hdepth)]

    def origin(q):
        return w_hbm.at[pl.ds((q % 2) * hdepth, hdepth), pl.ds((q // 2) * 128, 128)]

    def w_out(slot, q):
        src = origin(q) if slot < 3 else place(2, q)
        return remote(src, place(slot, q), w_send.at[slot - 1, q], w_recv.at[slot - 1, q],
                      ((far if slot == 2 else xn), y))

    def w_wait(slot, q):
        w_out(slot, q).wait_recv()

    own_loads = [pltpu.make_async_copy(origin(q), place(0, q), w_load.at[q]) for q in range(4)]
    for q in range(4):
        go(None, w_out(1, q))
        go(None, w_out(2, q))
    for one in own_loads:
        one.start()

    scale = DH ** (-0.25)

    def cols(h):
        return pl.ds(pl.multiple_of(h * DH, DH), DH)

    def feature_map(ref, h):
        t = ref[:, cols(h)]
        tf = t.astype(f32)
        norm = jnp.sum(tf * tf, axis=-1, keepdims=True) * (0.5 * scale * scale * LOG2E)
        proj = jnp.dot(jnp.concatenate([t, t], axis=1), fhl[h], preferred_element_type=f32)
        return jnp.exp2(proj - (norm + 0.5 * math.log2(M))).astype(bf16)

    zrow = lax.broadcasted_iota(jnp.int32, (TAIL, M), 0)
    hi_row = zrow % 8 < 4
    first = zrow < 8

    def narrow(s):
        tail = s[PER * DH :]
        tail = tail + jnp.where(hi_row, pltpu.roll(tail, TAIL - 4, 0), pltpu.roll(tail, 4, 0))
        hi = tail.astype(bf16).astype(f32)
        tail = jnp.where(hi_row, hi, tail - hi)
        return jnp.concatenate([s[: PER * DH].astype(bf16), tail.astype(bf16)], axis=0)

    def key_states(gg):
        parts = []
        for i in range(PER):
            h = PER * gg + i
            f = f_ref[h] * (scale * LOG2E)
            hi = f.astype(bf16)
            fhl[h, :DH] = hi
            fhl[h, DH:] = (f - hi.astype(f32)).astype(bf16)
            kf[h] = feature_map(k_ref, h)
            vt[h, :DH] = v_ref[:, cols(h)].T
            vt[h, DH:] = jnp.ones((TAIL, tok), bf16)
            parts.append(jnp.dot(vt[h], kf[h], preferred_element_type=f32))
        tail = jnp.where(hi_row, jnp.where(first, parts[0][DH:], parts[1][DH:]), 0.0)
        return jnp.concatenate([p[:DH] for p in parts] + [tail], axis=0)

    for one in loads[:3]:
        one.wait()

    def sb_copy(g):
        return remote(sbsend.at[g], sibst.at[g], sb_send.at[g], sb_recv.at[g], (sib, y))

    @pl.loop(0, GROUPS)
    def _(g):
        sbsend[g] = narrow(key_states(GROUPS * (1 - c) + g))
        sb_copy(g).start()

    def x_copy(i):
        return remote(xsend.at[i], xrecv.at[i], x_send.at[i], x_recv.at[i], (xn, y))

    @pl.loop(0, GROUPS)
    def _(i):
        g = (2 * (1 - x) + i) % GROUPS
        own32[g] = key_states(GROUPS * c + g)
        sb_copy(g).wait_recv()

        @pl.when(i < 2)
        def _():
            xsend[i] = narrow(own32[g] + sibst[g].astype(f32))
            x_copy(i).start()

    loads[3].wait()
    lower = (lax.broadcasted_iota(jnp.int32, (tok, tok), 1)
             <= lax.broadcasted_iota(jnp.int32, (tok, tok), 0))

    def across(a, b):
        return lax.dot_general(a, b, (((1,), (1,)), ((), ())), preferred_element_type=f32)

    def local_heads(start, stop):
        @pl.loop(start, stop)
        def _(h):
            qh = feature_map(q_ref, h)
            qf[h] = qh
            scores = jnp.where(lower, across(qh, kf[h]), 0.0).astype(bf16)
            both[h] = across(scores, vt[h])

    before = jnp.where(z == 0, heads // 4, heads)
    local_heads(0, before)

    at_x0, at_x1 = (x == 0).astype(f32), (x == 1).astype(f32)
    at_c0, at_c1 = (c == 0).astype(f32), (c == 1).astype(f32)

    def sp_copy(g):
        return remote(sbp.at[g], prior.at[GROUPS * c + g], sp_send.at[g], sp_recv.at[g], (sib, y))

    def sp_arrived(g):
        remote(sbp.at[g], prior.at[GROUPS * (1 - c) + g], sp_send.at[g], sp_recv.at[g],
               (sib, y)).wait_recv()

    def put_priors(g, base):
        sbp[g] = narrow(base + at_c0 * own32[g])
        sp_copy(g).start()
        prior[GROUPS * c + g] = narrow(base + at_c1 * sibst[g].astype(f32))

    for i in range(2):
        g = 2 * x + i
        x_copy(i).wait_recv()
        hop = remote(back.at[i], below.at[i], z_send.at[i], z_recv.at[i], (up, y))

        @pl.when(has_down)
        def _():
            hop.wait_recv()

        @pl.when(z == 0)
        def _():
            below[i] = jnp.zeros(below.shape[1:], bf16)

        chip = own32[g] + sibst[g].astype(f32)
        under = below[i].astype(f32)
        theirs = xrecv[i].astype(f32)

        @pl.when(has_up)
        def _():
            back[i] = narrow(under + chip + theirs)
        go(has_up, hop)
        xpsend[i] = narrow(under + at_x0 * chip)
        go(None, remote(xpsend.at[i], xprior.at[i], xp_send.at[i], xp_recv.at[i], (xn, y)))
        put_priors(g, under + at_x1 * theirs)

    local_heads(before, heads)
    w_wait(2, 0)
    go(None, w_out(3, 0))

    for i in range(2):
        g = 2 * (1 - x) + i
        remote(xpsend.at[i], xprior.at[i], xp_send.at[i], xp_recv.at[i], (xn, y)).wait_recv()
        put_priors(g, xprior[i].astype(f32))

    def finish(gg):
        tail = prior[gg, PER * DH :]
        for i in range(PER):
            h = PER * gg + i
            p = jnp.concatenate([prior[gg, i * DH : (i + 1) * DH], tail], axis=0)
            here, old = both[h], across(qf[h], p)
            at = DH + 8 * i
            den = here[:, DH : DH + 1] + old[:, at : at + 1] + old[:, at + 4 : at + 5]
            attb[0, :, cols(h)] = ((here[:, :DH] + old[:, :DH]) / den).astype(bf16)

    @pl.loop(0, GROUPS)
    def _(i):
        finish(GROUPS * c + (2 * x + i) % GROUPS)

    @pl.loop(0, GROUPS)
    def _(i):
        g = (2 * x + i) % GROUPS
        sp_arrived(g)
        finish(GROUPS * (1 - c) + g)

    att_sib = remote(attb.at[0], attb.at[1], at_send.at[0], at_recv.at[0], (sib, y))

    def att_z(j):
        return remote(attb.at[0, pl.ds(j * htok, htok)], attb.at[2 + j, pl.ds(0, htok)],
                      at_send.at[1 + j], at_recv.at[1 + j], (pz, y))

    def att_fwd(j):
        return remote(attb.at[2 + j, pl.ds(0, htok)], attb.at[2 + j, pl.ds(htok, htok)],
                      at_send.at[3 + j], at_recv.at[3 + j], (sib, y))

    go(None, att_z(0))
    go(None, att_z(1))
    go(None, att_sib)

    keeps_low = y == z // 2

    def p_copy(kk, t):
        return remote(psend.at[kk, t], precv.at[kk, t], p_send.at[kk, t], p_recv.at[kk, t],
                      (me, 1 - y))

    def item(hh, t):
        piece = jnp.dot(attb[t], wbuf[hh], preferred_element_type=f32)
        kk = hh % 4
        keep = (hh // 4 == 0) == keeps_low

        @pl.when(keep)
        def _():
            acc[kk, t] = piece

        @pl.when(jnp.logical_not(keep))
        def _():
            psend[kk, t] = piece.astype(bf16)
            p_copy(kk, t).start()

    def items(first_hh, count, t):
        @pl.loop(first_hh, first_hh + count)
        def _(hh):
            item(hh, t)

    def tokens(hh, first_t, count):
        @pl.loop(first_t, first_t + count)
        def _(t):
            item(hh, t)

    def block_of(kk, zz, cc):
        xs = jnp.where(kk // 2 == 0, x, 1 - x)
        return ((zz * 2 + xs) * 2 + cc) * 2 + kk % 2

    def o_sib(kk):
        return remote(osend.at[kk, 0], obuf.at[block_of(kk, z % 2, c)],
                      o_send.at[kk, 0], o_recv.at[kk, 0], (sib, y))

    def o_pair(kk, j, other):
        slot = 1 + 2 * j + other
        return remote(osend.at[kk, 1 + j, pl.ds(other * htok, htok)],
                      obuf.at[block_of(kk, z % 2, c), pl.ds(j * htok, htok)],
                      o_send.at[kk, slot], o_recv.at[kk, slot], ((pz, pzsib)[other], y))

    def final(kk, t):
        p_copy(kk, t).wait_recv()
        whole = (acc[kk, t] + precv[kk, t].astype(f32)).astype(bf16)
        if t == 0:
            obuf[block_of(kk, z % 2, c)] = whole
        elif t == 1:
            osend[kk, 0] = whole
            o_sib(kk).start()
        else:
            osend[kk, t - 1] = whole
            o_pair(kk, t - 2, 0).start()
            o_pair(kk, t - 2, 1).start()

    def finals(cond, first_kk, count, ts):
        @pl.when(cond)
        def _():
            @pl.loop(first_kk, first_kk + count)
            def _(kk):
                for t in ts:
                    final(kk, t)

    for one in own_loads:
        one.wait()
    w_wait(2, 1)
    go(None, w_out(3, 1))
    for q in range(4):
        w_wait(1, q)
    items(0, 4, 0)
    att_sib.wait_recv()
    items(0, 4, 1)
    tokens(4, 0, 2)
    w_wait(2, 2)
    go(None, w_out(3, 2))
    att_z(0).wait_recv()
    go(None, att_fwd(0))
    w_wait(2, 3)
    go(None, w_out(3, 3))
    tokens(5, 0, 2)
    att_fwd(0).wait_recv()
    items(0, 6, 2)
    finals(keeps_low, 0, 4, (2, 0, 1))
    keeps_high = jnp.logical_not(keeps_low)
    w_wait(3, 0)
    w_wait(3, 1)
    tokens(6, 0, 3)
    finals(keeps_high, 0, 2, (2, 0, 1))
    att_z(1).wait_recv()
    go(None, att_fwd(1))
    att_fwd(1).wait_recv()
    items(0, 7, 3)
    w_wait(3, 2)
    w_wait(3, 3)

    @pl.loop(0, 4)
    def _(i):
        item(7, 3 - i)
    finals(keeps_low, 0, 4, (3,))
    finals(keeps_high, 0, 2, (3,))
    finals(keeps_high, 2, 2, (3, 2, 1, 0))

    def show(block):
        out_ref[:, pl.ds(pl.multiple_of(block * 128, 128), 128)] = obuf[block]

    @pl.loop(0, 4)
    def _(kk):
        show(block_of(kk, z % 2, c))
        o_sib(kk).wait_recv()
        show(block_of(kk, z % 2, 1 - c))
        o_pair(kk, 0, 0).wait_recv()
        o_pair(kk, 1, 0).wait_recv()
        show(block_of(kk, 1 - z % 2, c))
        o_pair(kk, 0, 1).wait_recv()
        o_pair(kk, 1, 1).wait_recv()
        show(block_of(kk, 1 - z % 2, 1 - c))
        for t in range(4):
            p_copy(kk, t).wait_send()
        o_sib(kk).wait_send()
        for j in range(2):
            o_pair(kk, j, 0).wait_send()
            o_pair(kk, j, 1).wait_send()

    @pl.loop(0, GROUPS)
    def _(g):
        sb_copy(g).wait_send()
        sp_copy(g).wait_send()
    for i in range(2):
        x_copy(i).wait_send()
    for cond, copy in started:
        if cond is None:
            copy.wait_send()
        else:
            pl.when(cond)(copy.wait_send)


def fused(queries, keys, values, features, weight):
    tok, columns = queries.shape
    heads = features.shape[0]
    depth = weight.shape[0]
    f32, bf16 = jnp.float32, jnp.bfloat16
    vmem = pltpu.VMEM
    dma = pltpu.SemaphoreType.DMA
    rows = PER * DH + TAIL
    return pl.pallas_call(
        kernel_body,
        out_shape=jax.ShapeDtypeStruct((tok, columns), bf16),
        in_specs=[pl.BlockSpec(memory_space=pl.ANY)] * 5,
        out_specs=pl.BlockSpec(memory_space=pltpu.VMEM),
        scratch_shapes=[
            vmem((tok, columns), bf16),
            vmem((tok, columns), bf16),
            vmem((tok, columns), bf16),
            vmem(features.shape, f32),
            vmem((8, depth, 128), bf16),
            vmem((heads, 2 * DH, M), bf16),
            vmem((heads, tok, M), bf16),
            vmem((heads, tok, M), bf16),
            vmem((heads, DH + TAIL, tok), bf16),
            vmem((heads, tok, DH + TAIL), f32),
            vmem((GROUPS, rows, M), f32),
            vmem((GROUPS, rows, M), bf16),
            vmem((GROUPS, rows, M), bf16),
            vmem((2, rows, M), bf16),
            vmem((2, rows, M), bf16),
            vmem((2, rows, M), bf16),
            vmem((2, rows, M), bf16),
            vmem((2, rows, M), bf16),
            vmem((2, rows, M), bf16),
            vmem((2 * GROUPS, rows, M), bf16),
            vmem((GROUPS, rows, M), bf16),
            vmem((4, tok, columns), bf16),
            vmem((4, 4, tok, 128), f32),
            vmem((4, 4, tok, 128), bf16),
            vmem((4, 4, tok, 128), bf16),
            vmem((4, 3, tok, 128), bf16),
            vmem((16, tok, 128), bf16),
            dma((4,)), dma((4,)), dma((3, 4)), dma((3, 4)),
            dma((GROUPS,)), dma((GROUPS,)), dma((2,)), dma((2,)), dma((2,)), dma((2,)),
            dma((2,)), dma((2,)), dma((GROUPS,)), dma((GROUPS,)), dma((5,)), dma((5,)),
            dma((4, 4)), dma((4, 4)), dma((4, 5)), dma((4, 5)),
        ],
        compiler_params=pltpu.CompilerParams(
            collective_id=0, has_side_effects=True, vmem_limit_bytes=60 << 20),
    )(queries, keys, values, features, weight)


def shards(queries, keys, values, features, output_proj_weight):
    fits = (
        lax.axis_size("seq") == PLANE * DEPTH
        and lax.axis_size("head") == 2
        and features.shape == (2 * PER * GROUPS, DH, M)
        and queries.shape == (256, 2048)
        and output_proj_weight.shape == (2048, 256)
    )
    step = fused if fits else plain
    return step(queries, keys, values, features, output_proj_weight)


def solution(mesh):
    in_specs = (
        P("seq", "head"),
        P("seq", "head"),
        P("seq", "head"),
        P("head", None, None),
        P("head", "seq"),
    )
    return jax.shard_map(
        shards, mesh=mesh, in_specs=in_specs, out_specs=P("seq", "head"), check_vma=False
    )
```

```python
import math

import jax
import jax.numpy as jnp
from jax import lax
from jax.experimental import pallas as pl
from jax.experimental.pallas import tpu as pltpu
from jax.sharding import PartitionSpec as P

DH = 128
M = 256
HIGH = lax.Precision.HIGHEST


def feature_map(x, direction):
    x = x * DH ** (-0.25)
    proj = jnp.einsum("htd,hdm->htm", x, direction, precision=HIGH)
    return jnp.exp(proj - 0.5 * jnp.sum(x * x, axis=-1, keepdims=True)) / math.sqrt(M)


def plain(queries, keys, values, features, output_proj_weight):
    tok_rows = queries.shape[0]
    local_heads = features.shape[0]
    devices, here = lax.axis_size("seq"), lax.axis_index("seq")
    halves, half = lax.axis_size("head"), lax.axis_index("head")

    def split_heads(arr):
        return arr.astype(jnp.float32).reshape(tok_rows, local_heads, DH).transpose(1, 0, 2)

    kf = feature_map(split_heads(keys), features)
    v = split_heads(values)
    v = jnp.concatenate([v, jnp.ones((local_heads, tok_rows, 8), jnp.float32)], axis=2)
    state = jnp.einsum("htp,htk->hpk", v, kf, precision=HIGH)
    states = lax.all_gather(state.astype(jnp.bfloat16), "seq")
    state, weight = lax.optimization_barrier((state, output_proj_weight))
    whole = lax.all_gather(weight, "seq", axis=1, tiled=True)
    qf = feature_map(split_heads(queries), features)
    lower = jnp.tril(jnp.ones((tok_rows, tok_rows), jnp.float32))
    scores = jnp.einsum("htm,hsm->hts", qf, kf, precision=HIGH) * lower
    both = jnp.einsum("hts,hsd->htd", scores, v, precision=HIGH)
    earlier = (jnp.arange(devices) < here)[:, None, None, None]
    prior = jnp.sum(jnp.where(earlier, states.astype(jnp.float32), 0.0), axis=0)
    both = both + jnp.einsum("htk,hpk->htp", qf, prior, precision=HIGH)
    attended = both[:, :, :DH] / both[:, :, DH : DH + 1]
    attended = attended.transpose(1, 0, 2).reshape(tok_rows, local_heads * DH).astype(jnp.bfloat16)
    partial = jnp.dot(attended, whole, preferred_element_type=jnp.float32)
    width = partial.shape[1] // halves
    total = lax.dynamic_slice_in_dim(partial, half * width, width, 1)
    for shift in range(1, halves):
        theirs = lax.rem(half + shift, halves)
        piece = lax.dynamic_slice_in_dim(partial, theirs * width, width, 1).astype(jnp.bfloat16)
        got = lax.ppermute(piece, "head", [(i, (i + shift) % halves) for i in range(halves)])
        total = total + got.astype(jnp.float32)
    return total.astype(jnp.bfloat16)


PLANE, DEPTH = 4, 4
HALF = 8
OWN = 4
TAIL = 16
WQ = 8
CHUNKS = 4
LOG2E = math.log2(math.e)


def kernel_body(q_hbm, k_hbm, v_hbm, f_hbm, w_hbm, out_ref, q_ref, k_ref, v_ref, f_ref, wbuf, fhl,
                kf, qf, vt, both, own32, sibst, sbsend, xsend, xrecv, below, back, xpsend, xprior,
                prior, sbp, attb, attp, acc, accp, psend, precv, qsend, qrecv, osend, opsend, obuf,
                in_sem, w_load, w_send, w_recv, sb_send, sb_recv, x_send, x_recv, z_send, z_recv,
                xp_send, xp_recv, sp_send, sp_recv, at_send, at_recv, p_send, p_recv,
                pp_send, pp_recv, o_send, o_recv, op_send, op_recv):
    f32, bf16 = jnp.float32, jnp.bfloat16
    tok = q_ref.shape[0]
    ctok = tok // CHUNKS
    heads = f_ref.shape[0]
    qrows = w_hbm.shape[0] // 4
    me, y = lax.axis_index("seq"), lax.axis_index("head")
    z, x, c = me // PLANE, (me // 2) % 2, me % 2
    sib, xn, up, down = me + 1 - 2 * c, me + 2 - 4 * x, me + PLANE, me - PLANE
    pz = me + PLANE - 2 * PLANE * (z % 2)
    pzsib = pz + 1 - 2 * c
    far = me + 2 * PLANE - 4 * PLANE * (z // 2)
    has_up, has_down = z < DEPTH - 1, z > 0

    loads = [pltpu.make_async_copy(a, b, in_sem.at[i]) for i, (a, b) in enumerate(
        ((k_hbm, k_ref), (f_hbm, f_ref), (v_hbm, v_ref), (q_hbm, q_ref)))]
    for one in loads:
        one.start()
    barrier = pltpu.get_barrier_semaphore()

    def greet(device):
        pl.semaphore_signal(barrier, inc=1, device_id=device, device_id_type=pl.DeviceIdType.MESH)

    for device in ((sib, y), (xn, y), (me, 1 - y), (far, y), (pzsib, y)):
        greet(device)

    @pl.when(has_up)
    def _():
        greet((up, y))

    @pl.when(has_down)
    def _():
        greet((down, y))

    pl.semaphore_wait(barrier, 5 + has_up.astype(jnp.int32) + has_down.astype(jnp.int32))

    def remote(src, dst, ssem, rsem, device):
        return pltpu.make_async_remote_copy(
            src_ref=src, dst_ref=dst, send_sem=ssem, recv_sem=rsem, device_id=(device, y),
            device_id_type=pl.DeviceIdType.MESH)

    def place(slot, q):
        return wbuf.at[2 * slot + q // 4, pl.ds((q % 4) * qrows, qrows)]

    def origin(q):
        return w_hbm.at[pl.ds((q % 4) * qrows, qrows), pl.ds((q // 4) * 128, 128)]

    def w_out(slot, q):
        src = origin(q) if slot < 3 else place(2, q)
        return remote(src, place(slot, q), w_send.at[slot - 1, q], w_recv.at[slot - 1, q],
                      far if slot == 2 else xn)

    def w_wait(slot, *qs):
        for q in qs:
            w_out(slot, q).wait_recv()

    def w_go(slot, cond, *qs):
        def start():
            for q in qs:
                w_out(slot, q).start()
        if cond is None:
            start()
        else:
            pl.when(cond)(start)

    def forward(*qs):
        for q in qs:
            w_out(2, q).wait_recv()
            w_out(3, q).start()

    own_loads = [pltpu.make_async_copy(origin(q), place(0, q), w_load.at[q]) for q in range(WQ)]
    w_go(1, None, 0)
    w_go(2, None, 0, 1)
    w_go(2, z == 3, 2, 3, 4, 5, 6, 7)

    scale = DH ** (-0.25)

    def cols(h):
        return pl.ds(pl.multiple_of(h * DH, DH), DH)

    def feature_map(ref, h):
        t = ref[:, cols(h)]
        tf = t.astype(f32)
        norm = jnp.sum(tf * tf, axis=-1, keepdims=True) * (0.5 * scale * scale * LOG2E)
        proj = jnp.dot(jnp.concatenate([t, t], axis=1), fhl[h], preferred_element_type=f32)
        return jnp.exp2(proj - (norm + 0.5 * math.log2(M))).astype(bf16)

    hi_row = lax.broadcasted_iota(jnp.int32, (TAIL, M), 0) < TAIL // 2

    def narrow(s):
        tail = s[DH:]
        tail = tail + pltpu.roll(tail, TAIL // 2, 0)
        hi = tail.astype(bf16).astype(f32)
        tail = jnp.where(hi_row, hi, tail - hi)
        return jnp.concatenate([s[:DH].astype(bf16), tail.astype(bf16)], axis=0)

    def key_state(h):
        f = f_ref[h] * (scale * LOG2E)
        hi = f.astype(bf16)
        fhl[h, :DH] = hi
        fhl[h, DH:] = (f - hi.astype(f32)).astype(bf16)
        kf[h] = feature_map(k_ref, h)
        vt[h, :DH] = v_ref[:, cols(h)].T
        vt[h, DH:] = jnp.ones((TAIL, tok), bf16)
        s = jnp.dot(vt[h], kf[h], preferred_element_type=f32)
        return jnp.concatenate([s[:DH], jnp.where(hi_row, s[DH:], 0.0)], axis=0)

    def sb_copy(g):
        return remote(sbsend.at[g], sibst.at[g], sb_send.at[g], sb_recv.at[g], sib)

    def x_copy(i):
        return remote(xsend.at[i], xrecv.at[i], x_send.at[i], x_recv.at[i], xn)

    for one in loads[:3]:
        one.wait()

    @pl.loop(0, OWN + 1)
    def _(i):
        @pl.when(i < OWN)
        def _():
            for g in (OWN * (1 - x) + i, OWN * x + i):
                sbsend[g] = key_state(HALF * (1 - c) + g)
                sb_copy(g).start()
                own32[g] = key_state(HALF * c + g)

        @pl.when(i > 0)
        def _():
            g = OWN * (1 - x) + i - 1
            sb_copy(g).wait_recv()
            sb_copy(OWN * x + i - 1).wait_recv()
            xsend[i - 1] = narrow(own32[g] + sibst[g])
            x_copy(i - 1).start()

    w_go(1, z > 0, 1)
    w_go(1, z > 1, 2)
    w_go(1, z > 2, 3)
    w_go(2, z == 2, 2, 3)
    for one in own_loads:
        one.start()
    loads[3].wait()
    lower = (lax.broadcasted_iota(jnp.int32, (tok, tok), 1)
             <= lax.broadcasted_iota(jnp.int32, (tok, tok), 0))

    def across(a, b):
        return lax.dot_general(a, b, (((1,), (1,)), ((), ())), preferred_element_type=f32)

    def local_heads(start, stop):
        @pl.loop(start, stop)
        def _(h):
            qh = feature_map(q_ref, h)
            qf[h] = qh
            scores = jnp.where(lower, across(qh, kf[h]), 0.0).astype(bf16)
            both[h] = across(scores, vt[h])

    before = jnp.where(z == 0, 0, heads)
    local_heads(0, before)

    at_x0, at_x1 = (x == 0).astype(f32), (x == 1).astype(f32)
    at_c0, at_c1 = (c == 0).astype(f32), (c == 1).astype(f32)

    def sp_copy(g):
        return remote(sbp.at[g], prior.at[HALF * c + g], sp_send.at[g], sp_recv.at[g], sib)

    def put_priors(g, base):
        sbp[g] = base + at_c0 * own32[g]
        sp_copy(g).start()
        prior[HALF * c + g] = base + at_c1 * sibst[g]

    def z_copy(i):
        return remote(back.at[i], below.at[i], z_send.at[i], z_recv.at[i], up)

    def xp_copy(i):
        return remote(xpsend.at[i], xprior.at[i], xp_send.at[i], xp_recv.at[i], xn)

    @pl.loop(0, OWN)
    def _(i):
        g = OWN * x + i
        x_copy(i).wait_recv()

        @pl.when(has_down)
        def _():
            z_copy(i).wait_recv()

        @pl.when(z == 0)
        def _():
            below[i] = jnp.zeros(below.shape[1:], bf16)

        chip = own32[g] + sibst[g]
        under = below[i].astype(f32)
        theirs = xrecv[i].astype(f32)

        @pl.when(has_up)
        def _():
            back[i] = narrow(under + chip + theirs)
            z_copy(i).start()
        xpsend[i] = narrow(under + at_x0 * chip)
        xp_copy(i).start()
        put_priors(g, under + at_x1 * theirs)

    w_go(1, z == 0, 1)
    w_go(1, z <= 1, 2)
    w_go(1, z <= 2, 3)
    w_go(1, None, 4, 5, 6, 7)
    w_go(2, z < 2, 2, 3)
    w_go(2, jnp.logical_or(z == 1, z == 2), 4, 5, 6, 7)
    local_heads(before, heads)

    def finish(h):
        p = prior[h]
        hi = p.astype(bf16)
        lo = (p - hi.astype(f32)).astype(bf16)
        twice = jnp.concatenate([qf[h], qf[h]], axis=1)
        total = both[h] + across(twice, jnp.concatenate([hi, lo], axis=1))
        at = DH + TAIL // 2
        spare = total[:, at : at + 1] - both[h, :, at : at + 1]
        den = total[:, DH : DH + 1] + spare
        attb[0, :, cols(h)] = (total[:, :DH] / den).astype(bf16)

    def finish_group(first):
        @pl.loop(first, first + OWN)
        def _(g):
            finish(HALF * c + g)

        @pl.loop(first, first + OWN)
        def _(g):
            remote(sbp.at[g], prior.at[HALF * (1 - c) + g], sp_send.at[g], sp_recv.at[g],
                   sib).wait_recv()
            finish(HALF * (1 - c) + g)

    finish_group(OWN * x)

    @pl.loop(0, OWN)
    def _(i):
        xp_copy(i).wait_recv()
        put_priors(OWN * (1 - x) + i, xprior[i].astype(f32))

    finish_group(OWN * (1 - x))

    def att_z(j):
        return remote(attb.at[0, pl.ds(j * ctok, ctok)], attp.at[j, pl.ds(0, ctok)],
                      at_send.at[j], at_recv.at[j], pz)

    def att_fwd(j):
        return remote(attp.at[j, pl.ds(0, ctok)], attp.at[j, pl.ds(ctok, ctok)],
                      at_send.at[CHUNKS + j], at_recv.at[CHUNKS + j], sib)

    att_sib = remote(attb.at[0], attb.at[1], at_send.at[2 * CHUNKS], at_recv.at[2 * CHUNKS], sib)
    for j in range(CHUNKS):
        att_z(j).start()
        w_go(2, z == 0, 4 + j)
    att_sib.start()

    keeps_low = y == z // 2
    keeps_high = jnp.logical_not(keeps_low)

    def p_copy(kk, t):
        return pltpu.make_async_remote_copy(
            src_ref=psend.at[kk, t], dst_ref=precv.at[kk, t], send_sem=p_send.at[kk, t],
            recv_sem=p_recv.at[kk, t], device_id=(me, 1 - y), device_id_type=pl.DeviceIdType.MESH)

    def q_copy(kk, j):
        return pltpu.make_async_remote_copy(
            src_ref=qsend.at[kk, j], dst_ref=qrecv.at[kk, j], send_sem=pp_send.at[kk, j],
            recv_sem=pp_recv.at[kk, j], device_id=(me, 1 - y), device_id_type=pl.DeviceIdType.MESH)

    def item(src, hh, t, sums, out, copy):
        piece = jnp.dot(src[t], wbuf[hh], preferred_element_type=f32)
        kk = hh % 4
        keep = (hh // 4 == 0) == keeps_low

        @pl.when(keep)
        def _():
            sums[kk, t] = piece

        @pl.when(jnp.logical_not(keep))
        def _():
            out[kk, t] = piece.astype(bf16)
            copy(kk, t).start()

    def large(first_hh, count, t):
        @pl.loop(first_hh, first_hh + count)
        def _(hh):
            item(attb, hh, t, acc, psend, p_copy)

    def small(first_hh, count, first_j, many=1):
        @pl.loop(0, count * many)
        def _(i):
            item(attp, first_hh + i % count, first_j + i // count, accp, qsend, q_copy)

    def block_of(kk, zz, cc):
        xs = jnp.where(kk // 2 == 0, x, 1 - x)
        return ((zz * 2 + xs) * 2 + cc) * 2 + kk % 2

    def o_copy(kk):
        return remote(osend.at[kk], obuf.at[block_of(kk, z % 2, c)], o_send.at[kk], o_recv.at[kk],
                      sib)

    def op_copy(kk, j, other):
        return remote(opsend.at[kk, j, pl.ds(other * ctok, ctok)],
                      obuf.at[block_of(kk, z % 2, c), pl.ds(j * ctok, ctok)],
                      op_send.at[kk, j, other], op_recv.at[kk, j, other], (pz, pzsib)[other])

    def final_large(cond, first_kk, count):
        @pl.when(cond)
        def _():
            @pl.loop(first_kk, first_kk + count)
            def _(kk):
                p_copy(kk, 1).wait_recv()
                osend[kk] = (acc[kk, 1] + precv[kk, 1].astype(f32)).astype(bf16)
                o_copy(kk).start()
                p_copy(kk, 0).wait_recv()
                obuf[block_of(kk, z % 2, c)] = (acc[kk, 0] + precv[kk, 0].astype(f32)).astype(bf16)

    def final_small(cond, first_kk, count, first_j, many=1):
        @pl.when(cond)
        def _():
            @pl.loop(0, count * many)
            def _(i):
                kk, j = first_kk + i % count, first_j + i // count
                q_copy(kk, j).wait_recv()
                opsend[kk, j] = (accp[kk, j] + qrecv[kk, j].astype(f32)).astype(bf16)
                op_copy(kk, j, 0).start()
                op_copy(kk, j, 1).start()

    def take(j):
        att_z(j).wait_recv()
        att_fwd(j).start()

    forward(0, 1, 2, 3)
    for one in own_loads:
        one.wait()
    large(0, 2, 0)
    att_sib.wait_recv()
    large(0, 2, 1)
    w_wait(1, *range(WQ))
    large(2, 2, 0)
    large(2, 2, 1)
    take(0)
    forward(4, 5)
    large(4, 1, 0)
    large(4, 1, 1)
    take(1)
    att_fwd(0).wait_recv()
    small(0, 5, 0)
    final_large(keeps_low, 0, 4)
    att_fwd(1).wait_recv()
    small(0, 5, 1)
    forward(6)
    take(2)
    final_small(keeps_low, 0, 4, 0)
    att_fwd(2).wait_recv()
    small(0, 5, 2)
    forward(7)
    large(5, 1, 0)
    large(5, 1, 1)
    small(5, 1, 0, 3)
    final_small(keeps_low, 0, 4, 1)
    w_wait(3, 0, 1, 2, 3)
    large(6, 1, 0)
    large(6, 1, 1)
    small(6, 1, 0, 3)
    final_small(keeps_low, 0, 4, 2)
    final_large(keeps_high, 0, 3)
    final_small(keeps_high, 0, 3, 0, 3)
    take(3)
    att_fwd(3).wait_recv()
    small(0, 7, 3)
    final_small(keeps_low, 0, 4, 3)
    w_wait(3, 4, 5, 6, 7)
    small(7, 1, 0, 4)
    large(7, 1, 1)
    large(7, 1, 0)
    final_small(keeps_high, 0, 3, 3)
    final_small(keeps_high, 3, 1, 0, 4)
    final_large(keeps_high, 3, 1)

    def show(block):
        out_ref[:, pl.ds(pl.multiple_of(block * 128, 128), 128)] = obuf[block]

    @pl.loop(0, 4)
    def _(kk):
        show(block_of(kk, z % 2, c))
        o_copy(kk).wait_recv()
        show(block_of(kk, z % 2, 1 - c))
        for other in range(2):
            for j in range(CHUNKS):
                op_copy(kk, j, other).wait_recv()
            show(block_of(kk, 1 - z % 2, c if other == 0 else 1 - c))
        for t in range(2):
            p_copy(kk, t).wait_send()
        o_copy(kk).wait_send()
        for j in range(CHUNKS):
            q_copy(kk, j).wait_send()
            for other in range(2):
                op_copy(kk, j, other).wait_send()

    @pl.loop(0, HALF)
    def _(g):
        sb_copy(g).wait_send()
        sp_copy(g).wait_send()

    @pl.loop(0, OWN)
    def _(i):
        x_copy(i).wait_send()
        xp_copy(i).wait_send()

        @pl.when(has_up)
        def _():
            z_copy(i).wait_send()
    for j in range(CHUNKS):
        att_z(j).wait_send()
        att_fwd(j).wait_send()
    att_sib.wait_send()
    for q in range(WQ):
        for slot in range(1, 4):
            w_out(slot, q).wait_send()


def fused(queries, keys, values, features, weight):
    tok, columns = queries.shape
    heads = features.shape[0]
    depth = weight.shape[0]
    f32, bf16 = jnp.float32, jnp.bfloat16
    vmem = pltpu.VMEM
    dma = pltpu.SemaphoreType.DMA
    rows = DH + TAIL
    part = tok // CHUNKS
    return pl.pallas_call(
        kernel_body,
        out_shape=jax.ShapeDtypeStruct((tok, columns), bf16),
        in_specs=[pl.BlockSpec(memory_space=pl.ANY)] * 5,
        out_specs=pl.BlockSpec(memory_space=pltpu.VMEM),
        scratch_shapes=[
            vmem((tok, columns), bf16),
            vmem((tok, columns), bf16),
            vmem((tok, columns), bf16),
            vmem(features.shape, f32),
            vmem((8, depth, 128), bf16),
            vmem((heads, 2 * DH, M), bf16),
            vmem((heads, tok, M), bf16),
            vmem((heads, tok, M), bf16),
            vmem((heads, rows, tok), bf16),
            vmem((heads, tok, rows), f32),
            vmem((HALF, rows, M), f32),
            vmem((HALF, rows, M), f32),
            vmem((HALF, rows, M), f32),
            vmem((OWN, rows, M), bf16),
            vmem((OWN, rows, M), bf16),
            vmem((OWN, rows, M), bf16),
            vmem((OWN, rows, M), bf16),
            vmem((OWN, rows, M), bf16),
            vmem((OWN, rows, M), bf16),
            vmem((heads, rows, M), f32),
            vmem((HALF, rows, M), f32),
            vmem((2, tok, columns), bf16),
            vmem((CHUNKS, 2 * part, columns), bf16),
            vmem((4, 2, tok, 128), f32),
            vmem((4, CHUNKS, 2 * part, 128), f32),
            vmem((4, 2, tok, 128), bf16),
            vmem((4, 2, tok, 128), bf16),
            vmem((4, CHUNKS, 2 * part, 128), bf16),
            vmem((4, CHUNKS, 2 * part, 128), bf16),
            vmem((4, tok, 128), bf16),
            vmem((4, CHUNKS, 2 * part, 128), bf16),
            vmem((16, tok, 128), bf16),
            dma((4,)), dma((WQ,)), dma((3, WQ)), dma((3, WQ)), dma((HALF,)), dma((HALF,)),
            dma((OWN,)), dma((OWN,)), dma((OWN,)), dma((OWN,)), dma((OWN,)), dma((OWN,)),
            dma((HALF,)), dma((HALF,)), dma((2 * CHUNKS + 1,)), dma((2 * CHUNKS + 1,)),
            dma((4, 2)), dma((4, 2)), dma((4, CHUNKS)), dma((4, CHUNKS)),
            dma((4,)), dma((4,)), dma((4, CHUNKS, 2)), dma((4, CHUNKS, 2)),
        ],
        compiler_params=pltpu.CompilerParams(
            collective_id=0, has_side_effects=True, vmem_limit_bytes=60 << 20),
    )(queries, keys, values, features, weight)


def shards(queries, keys, values, features, output_proj_weight):
    fits = (
        lax.axis_size("seq") == PLANE * DEPTH
        and lax.axis_size("head") == 2
        and features.shape == (2 * HALF, DH, M)
        and queries.shape == (256, 2048)
        and output_proj_weight.shape == (2048, 256)
    )
    step = fused if fits else plain
    return step(queries, keys, values, features, output_proj_weight)


def solution(mesh):
    in_specs = (
        P("seq", "head"),
        P("seq", "head"),
        P("seq", "head"),
        P("head", None, None),
        P("head", "seq"),
    )
    return jax.shard_map(
        shards, mesh=mesh, in_specs=in_specs, out_specs=P("seq", "head"), check_vma=False
    )
```

```python
import math

import jax
import jax.numpy as jnp
from jax import lax
from jax.experimental import pallas as pl
from jax.experimental.pallas import tpu as pltpu
from jax.sharding import PartitionSpec as P

DH = 128
M = 256
HIGH = lax.Precision.HIGHEST


def feature_map(x, direction):
    x = x * DH ** (-0.25)
    proj = jnp.einsum("htd,hdm->htm", x, direction, precision=HIGH)
    return jnp.exp(proj - 0.5 * jnp.sum(x * x, axis=-1, keepdims=True)) / math.sqrt(M)


def plain(queries, keys, values, features, output_proj_weight):
    tok_rows = queries.shape[0]
    local_heads = features.shape[0]
    devices, here = lax.axis_size("seq"), lax.axis_index("seq")
    halves, half = lax.axis_size("head"), lax.axis_index("head")

    def split_heads(arr):
        return arr.astype(jnp.float32).reshape(tok_rows, local_heads, DH).transpose(1, 0, 2)

    kf = feature_map(split_heads(keys), features)
    v = split_heads(values)
    v = jnp.concatenate([v, jnp.ones((local_heads, tok_rows, 8), jnp.float32)], axis=2)
    state = jnp.einsum("htp,htk->hpk", v, kf, precision=HIGH)
    states = lax.all_gather(state.astype(jnp.bfloat16), "seq")
    state, weight = lax.optimization_barrier((state, output_proj_weight))
    whole = lax.all_gather(weight, "seq", axis=1, tiled=True)
    qf = feature_map(split_heads(queries), features)
    lower = jnp.tril(jnp.ones((tok_rows, tok_rows), jnp.float32))
    scores = jnp.einsum("htm,hsm->hts", qf, kf, precision=HIGH) * lower
    both = jnp.einsum("hts,hsd->htd", scores, v, precision=HIGH)
    earlier = (jnp.arange(devices) < here)[:, None, None, None]
    prior = jnp.sum(jnp.where(earlier, states.astype(jnp.float32), 0.0), axis=0)
    both = both + jnp.einsum("htk,hpk->htp", qf, prior, precision=HIGH)
    attended = both[:, :, :DH] / both[:, :, DH : DH + 1]
    attended = attended.transpose(1, 0, 2).reshape(tok_rows, local_heads * DH).astype(jnp.bfloat16)
    partial = jnp.dot(attended, whole, preferred_element_type=jnp.float32)
    width = partial.shape[1] // halves
    total = lax.dynamic_slice_in_dim(partial, half * width, width, 1)
    for shift in range(1, halves):
        theirs = lax.rem(half + shift, halves)
        piece = lax.dynamic_slice_in_dim(partial, theirs * width, width, 1).astype(jnp.bfloat16)
        got = lax.ppermute(piece, "head", [(i, (i + shift) % halves) for i in range(halves)])
        total = total + got.astype(jnp.float32)
    return total.astype(jnp.bfloat16)


PLANE, DEPTH = 4, 4
HALF = 8
OWN = 4
TAIL = 16
WQ = 8
CHUNKS = 4
UNROLL = 4
LOG2E = math.log2(math.e)


def kernel_body(q_hbm, k_hbm, v_hbm, f_hbm, w_hbm, out_ref, q_ref, k_ref, v_ref, f_ref, wbuf, fhl,
                kf, qf, vt, both, own32, sibst, sbsend, xsend, xrecv, below, back, xpsend, xprior,
                prior, sbp, attb, attp, acc, accp, psend, precv, qsend, qrecv, osend, opsend, obuf,
                in_sem, w_load, w_send, w_recv, sb_send, sb_recv, x_send, x_recv, z_send, z_recv,
                xp_send, xp_recv, sp_send, sp_recv, at_send, at_recv, p_send, p_recv,
                pp_send, pp_recv, o_send, o_recv, op_send, op_recv):
    f32, bf16 = jnp.float32, jnp.bfloat16
    tok = q_ref.shape[0]
    ctok = tok // CHUNKS
    heads = f_ref.shape[0]
    qrows = w_hbm.shape[0] // 4
    me, y = lax.axis_index("seq"), lax.axis_index("head")
    z, x, c = me // PLANE, (me // 2) % 2, me % 2
    sib, xn, up, down = me + 1 - 2 * c, me + 2 - 4 * x, me + PLANE, me - PLANE
    pz = me + PLANE - 2 * PLANE * (z % 2)
    pzsib = pz + 1 - 2 * c
    far = me + 2 * PLANE - 4 * PLANE * (z // 2)
    has_up, has_down = z < DEPTH - 1, z > 0

    loads = [pltpu.make_async_copy(a, b, in_sem.at[i]) for i, (a, b) in enumerate(
        ((k_hbm, k_ref), (f_hbm, f_ref), (v_hbm, v_ref), (q_hbm, q_ref)))]
    for one in loads:
        one.start()
    barrier = pltpu.get_barrier_semaphore()

    def greet(device):
        pl.semaphore_signal(barrier, inc=1, device_id=device, device_id_type=pl.DeviceIdType.MESH)

    for device in ((sib, y), (xn, y), (me, 1 - y), (far, y), (pzsib, y)):
        greet(device)

    @pl.when(has_up)
    def _():
        greet((up, y))

    @pl.when(has_down)
    def _():
        greet((down, y))

    pl.semaphore_wait(barrier, 5 + has_up.astype(jnp.int32) + has_down.astype(jnp.int32))

    def remote(src, dst, ssem, rsem, device):
        return pltpu.make_async_remote_copy(
            src_ref=src, dst_ref=dst, send_sem=ssem, recv_sem=rsem, device_id=(device, y),
            device_id_type=pl.DeviceIdType.MESH)

    def place(slot, q):
        return wbuf.at[2 * slot + q // 4, pl.ds((q % 4) * qrows, qrows)]

    def origin(q):
        return w_hbm.at[pl.ds((q % 4) * qrows, qrows), pl.ds((q // 4) * 128, 128)]

    def w_out(slot, q):
        src = origin(q) if slot < 3 else place(2, q)
        return remote(src, place(slot, q), w_send.at[slot - 1, q], w_recv.at[slot - 1, q],
                      far if slot == 2 else xn)

    def w_wait(slot, *qs):
        for q in qs:
            w_out(slot, q).wait_recv()

    def w_go(slot, cond, *qs):
        def start():
            for q in qs:
                w_out(slot, q).start()
        if cond is None:
            start()
        else:
            pl.when(cond)(start)

    def forward(*qs):
        for q in qs:
            w_out(2, q).wait_recv()
            w_out(3, q).start()

    own_loads = [pltpu.make_async_copy(origin(q), place(0, q), w_load.at[q]) for q in range(WQ)]
    w_go(2, z == 0, 0, 1)
    w_go(1, z == 1, 0)
    w_go(2, z == 1, 0)
    w_go(1, z == 2, 0)
    w_go(2, z == 2, 0, 1, 2, 3, 4, 5)
    w_go(1, z == 3, 0)
    w_go(2, z == 3, 0, 1, 2, 3, 4)

    scale = DH ** (-0.25)

    def cols(h):
        return pl.ds(pl.multiple_of(h * DH, DH), DH)

    def feature_map(t, split):
        tf = t.astype(f32)
        norm = jnp.sum(tf * tf, axis=-1, keepdims=True) * (0.5 * scale * scale * LOG2E)
        proj = jnp.dot(jnp.concatenate([t, t], axis=1), split, preferred_element_type=f32)
        return jnp.exp2(proj - (norm + 0.5 * math.log2(M))).astype(bf16)

    hi_row = lax.broadcasted_iota(jnp.int32, (TAIL, M), 0) < TAIL // 2

    def narrow(s):
        tail = s[DH:]
        tail = tail + pltpu.roll(tail, TAIL // 2, 0)
        hi = tail.astype(bf16).astype(f32)
        tail = jnp.where(hi_row, hi, tail - hi)
        return jnp.concatenate([s[:DH].astype(bf16), tail.astype(bf16)], axis=0)

    def key_state(h):
        f = f_ref[h] * (scale * LOG2E)
        hi = f.astype(bf16)
        split = jnp.concatenate([hi, (f - hi.astype(f32)).astype(bf16)], axis=0)
        fhl[h] = split
        feats = feature_map(k_ref[:, cols(h)], split)
        kf[h] = feats
        flipped = jnp.concatenate([v_ref[:, cols(h)].T, jnp.ones((TAIL, tok), bf16)], axis=0)
        vt[h] = flipped
        s = jnp.dot(flipped, feats, preferred_element_type=f32)
        return jnp.concatenate([s[:DH], jnp.where(hi_row, s[DH:], 0.0)], axis=0)

    def sb_copy(g):
        return remote(sbsend.at[g], sibst.at[g], sb_send.at[g], sb_recv.at[g], sib)

    def x_copy(i):
        return remote(xsend.at[i], xrecv.at[i], x_send.at[i], x_recv.at[i], xn)

    for one in loads[:3]:
        one.wait()

    @pl.loop(0, OWN + 1)
    def _(i):
        @pl.when(i < OWN)
        def _():
            for g in (OWN * (1 - x) + i, OWN * x + i):
                sbsend[g] = key_state(HALF * (1 - c) + g)
                sb_copy(g).start()
                own32[g] = key_state(HALF * c + g)

        @pl.when(i > 0)
        def _():
            g = OWN * (1 - x) + i - 1
            sb_copy(g).wait_recv()
            sb_copy(OWN * x + i - 1).wait_recv()
            xsend[i - 1] = narrow(own32[g] + sibst[g])
            x_copy(i - 1).start()

    w_go(1, z == 1, 1)
    w_go(2, z == 1, 1, 2)
    w_go(1, z == 2, 1, 2)
    w_go(2, z == 2, 6)
    w_go(1, z == 3, 1, 2, 3)
    for one in own_loads:
        one.start()
    loads[3].wait()
    lower = (lax.broadcasted_iota(jnp.int32, (tok, tok), 1)
             <= lax.broadcasted_iota(jnp.int32, (tok, tok), 0))

    def across(a, b):
        return lax.dot_general(a, b, (((1,), (1,)), ((), ())), preferred_element_type=f32)

    def local_heads(start, stop):
        @pl.loop(start, stop)
        def _(i):
            some = [UNROLL * i + j for j in range(UNROLL)]
            qs = [feature_map(q_ref[:, cols(h)], fhl[h]) for h in some]
            scores = [jnp.where(lower, across(qh, kf[h]), 0.0).astype(bf16)
                      for h, qh in zip(some, qs)]
            sums = [across(s, vt[h]) for h, s in zip(some, scores)]
            for h, qh, total in zip(some, qs, sums):
                qf[h] = qh
                both[h] = total

    steps = heads // UNROLL
    before = jnp.where(z == 0, 0, steps)
    local_heads(0, before)

    at_x0, at_x1 = (x == 0).astype(f32), (x == 1).astype(f32)
    at_c0, at_c1 = (c == 0).astype(f32), (c == 1).astype(f32)

    def sp_copy(g):
        return remote(sbp.at[g], prior.at[HALF * c + g], sp_send.at[g], sp_recv.at[g], sib)

    def put_priors(g, base):
        sbp[g] = base + at_c0 * own32[g]
        sp_copy(g).start()
        prior[HALF * c + g] = base + at_c1 * sibst[g]

    def z_copy(i):
        return remote(back.at[i], below.at[i], z_send.at[i], z_recv.at[i], up)

    def xp_copy(i):
        return remote(xpsend.at[i], xprior.at[i], xp_send.at[i], xp_recv.at[i], xn)

    @pl.loop(0, OWN)
    def _(i):
        g = OWN * x + i
        x_copy(i).wait_recv()

        @pl.when(has_down)
        def _():
            z_copy(i).wait_recv()

        @pl.when(z == 0)
        def _():
            below[i] = jnp.zeros(below.shape[1:], bf16)

        chip = own32[g] + sibst[g]
        under = below[i].astype(f32)
        theirs = xrecv[i].astype(f32)

        @pl.when(has_up)
        def _():
            back[i] = narrow(under + chip + theirs)
            z_copy(i).start()
        xpsend[i] = narrow(under + at_x0 * chip)
        xp_copy(i).start()
        put_priors(g, under + at_x1 * theirs)

    w_go(1, z == 0, 0, 1, 2, 3, 4, 5)
    w_go(2, z == 0, 2)
    w_go(1, z == 1, 2, 3, 4, 5)
    w_go(2, z == 1, 3, 4, 5)
    w_go(1, z == 2, 3, 4, 5)
    w_go(2, z == 2, 7)
    w_go(1, z == 3, 4, 5)
    w_go(2, z == 3, 5, 6, 7)
    local_heads(before, steps)

    def finish(some):
        done = []
        for h in some:
            p = prior[h]
            hi = p.astype(bf16)
            lo = (p - hi.astype(f32)).astype(bf16)
            old = across(jnp.concatenate([qf[h], qf[h]], axis=1),
                         jnp.concatenate([hi, lo], axis=1))
            here, at = both[h], DH + TAIL // 2
            den = here[:, DH : DH + 1] + old[:, DH : DH + 1] + old[:, at : at + 1]
            done.append(((here[:, :DH] + old[:, :DH]) * (1.0 / den)).astype(bf16))
        for h, part in zip(some, done):
            attb[0, :, cols(h)] = part

    def finish_group(first):
        finish([HALF * c + first + i for i in range(OWN)])

        @pl.loop(first, first + OWN)
        def _(g):
            remote(sbp.at[g], prior.at[HALF * (1 - c) + g], sp_send.at[g], sp_recv.at[g],
                   sib).wait_recv()
        finish([HALF * (1 - c) + first + i for i in range(OWN)])

    finish_group(OWN * x)

    @pl.loop(0, OWN)
    def _(i):
        xp_copy(i).wait_recv()
        put_priors(OWN * (1 - x) + i, xprior[i].astype(f32))

    finish_group(OWN * (1 - x))

    def att_z(j):
        return remote(attb.at[0, pl.ds(j * ctok, ctok)], attp.at[j, pl.ds(0, ctok)],
                      at_send.at[j], at_recv.at[j], pz)

    def att_fwd(j):
        return remote(attp.at[j, pl.ds(0, ctok)], attp.at[j, pl.ds(ctok, ctok)],
                      at_send.at[CHUNKS + j], at_recv.at[CHUNKS + j], sib)

    att_sib = remote(attb.at[0], attb.at[1], at_send.at[2 * CHUNKS], at_recv.at[2 * CHUNKS], sib)
    w_go(2, z == 1, 6, 7)
    att_z(0).start()
    w_go(2, z == 0, 3)
    att_z(1).start()
    w_go(2, z == 0, 4)
    att_z(2).start()
    w_go(2, z == 0, 5)
    att_z(3).start()
    w_go(2, z == 0, 6, 7)
    att_sib.start()

    keeps_low = y == z // 2
    keeps_high = jnp.logical_not(keeps_low)

    def p_copy(kk, t):
        return pltpu.make_async_remote_copy(
            src_ref=psend.at[kk, t], dst_ref=precv.at[kk, t], send_sem=p_send.at[kk, t],
            recv_sem=p_recv.at[kk, t], device_id=(me, 1 - y), device_id_type=pl.DeviceIdType.MESH)

    def q_copy(kk, j):
        return pltpu.make_async_remote_copy(
            src_ref=qsend.at[kk, j], dst_ref=qrecv.at[kk, j], send_sem=pp_send.at[kk, j],
            recv_sem=pp_recv.at[kk, j], device_id=(me, 1 - y), device_id_type=pl.DeviceIdType.MESH)

    def item(src, hh, t, sums, out, copy):
        piece = jnp.dot(src[t], wbuf[hh], preferred_element_type=f32)
        kk = hh % 4
        keep = (hh // 4 == 0) == keeps_low

        @pl.when(keep)
        def _():
            sums[kk, t] = piece

        @pl.when(jnp.logical_not(keep))
        def _():
            out[kk, t] = piece.astype(bf16)
            copy(kk, t).start()

    def pair(src, slot, t, sums, out, copy):
        weight = jnp.concatenate([wbuf[2 * slot], wbuf[2 * slot + 1]], axis=1)
        piece = jnp.dot(src[t], weight, preferred_element_type=f32)
        first = 2 * (slot % 2)
        keep = (slot // 2 == 0) == keeps_low

        @pl.when(keep)
        def _():
            sums[first, t] = piece[:, :128]
            sums[first + 1, t] = piece[:, 128:]

        @pl.when(jnp.logical_not(keep))
        def _():
            for i in range(2):
                out[first + i, t] = piece[:, 128 * i : 128 * (i + 1)].astype(bf16)
                copy(first + i, t).start()

    def large_pair(slot):
        @pl.loop(0, 2)
        def _(t):
            pair(attb, slot, t, acc, psend, p_copy)

    def small_pair(slot, first_j, many=1):
        @pl.loop(first_j, first_j + many)
        def _(j):
            pair(attp, slot, j, accp, qsend, q_copy)

    def large(first_hh, count, t):
        @pl.loop(first_hh, first_hh + count)
        def _(hh):
            item(attb, hh, t, acc, psend, p_copy)

    def small(first_hh, count, first_j, many=1):
        @pl.loop(0, count * many)
        def _(i):
            item(attp, first_hh + i % count, first_j + i // count, accp, qsend, q_copy)

    def block_of(kk, zz, cc):
        xs = jnp.where(kk // 2 == 0, x, 1 - x)
        return ((zz * 2 + xs) * 2 + cc) * 2 + kk % 2

    def o_copy(kk):
        return remote(osend.at[kk], obuf.at[block_of(kk, z % 2, c)], o_send.at[kk], o_recv.at[kk],
                      sib)

    def op_copy(kk, j, other):
        return remote(opsend.at[kk, j, pl.ds(other * ctok, ctok)],
                      obuf.at[block_of(kk, z % 2, c), pl.ds(j * ctok, ctok)],
                      op_send.at[kk, j, other], op_recv.at[kk, j, other], (pz, pzsib)[other])

    def final_large(cond, first_kk, count):
        @pl.when(cond)
        def _():
            @pl.loop(first_kk, first_kk + count)
            def _(kk):
                p_copy(kk, 1).wait_recv()
                osend[kk] = (acc[kk, 1] + precv[kk, 1].astype(f32)).astype(bf16)
                o_copy(kk).start()
                p_copy(kk, 0).wait_recv()
                obuf[block_of(kk, z % 2, c)] = (acc[kk, 0] + precv[kk, 0].astype(f32)).astype(bf16)

    def final_small(cond, first_kk, count, first_j, many=1):
        @pl.when(cond)
        def _():
            @pl.loop(0, count * many)
            def _(i):
                kk, j = first_kk + i % count, first_j + i // count
                q_copy(kk, j).wait_recv()
                opsend[kk, j] = (accp[kk, j] + qrecv[kk, j].astype(f32)).astype(bf16)
                op_copy(kk, j, 0).start()
                op_copy(kk, j, 1).start()

    def take(j):
        att_z(j).wait_recv()
        att_fwd(j).start()

    def at_planes(cond, takes, forwards):
        @pl.when(cond)
        def _():
            for j in takes:
                take(j)
            forward(*forwards)

    w_go(1, None, 6, 7)
    for one in own_loads:
        one.wait()
    att_sib.wait_recv()
    large_pair(0)
    forward(0, 1, 2, 3)
    at_planes((z == 1) | (z == 2), (), (4, ))
    large(4, 1, 0)
    large(4, 1, 1)
    at_planes((z == 0), (), (4, ))
    take(0)
    take(1)
    att_fwd(0).wait_recv()
    att_fwd(1).wait_recv()
    w_wait(1, 0, 1, 2, 3, 4, 5, 6, 7)
    large_pair(1)
    at_planes((z == 3), (), (4, ))
    small_pair(0, 0, 2)
    at_planes((z == 0) | (z == 1) | (z == 2), (), (5, ))
    small(4, 1, 0, 2)
    at_planes((z == 3), (), (5, ))
    w_wait(3, 0, 1, 2, 3)
    large(6, 1, 0)
    large(6, 1, 1)
    small(6, 1, 0, 2)
    forward(6, 7)
    large(5, 1, 0)
    large(5, 1, 1)
    at_planes((z == 2), (2, ), ())
    small(5, 1, 0, 2)
    small_pair(1, 0, 2)
    at_planes((z == 0) | (z == 1) | (z == 3), (2, ), ())
    final_large(keeps_high, 0, 1)
    final_small(keeps_high, 0, 1, 0, 2)
    take(3)
    att_fwd(2).wait_recv()
    att_fwd(3).wait_recv()
    small_pair(1, 2, 2)
    final_large(keeps_high, 1, 1)
    final_small(keeps_high, 1, 1, 0, 2)
    final_large(keeps_low, 0, 4)
    final_small(keeps_low, 0, 4, 0, 2)
    small_pair(0, 2, 2)
    final_large(keeps_high, 2, 1)
    final_small(keeps_high, 2, 1, 0, 2)
    small(4, 3, 2, 2)
    final_small(keeps_high, 0, 3, 2, 2)
    w_wait(3, 4, 5, 6, 7)
    small(7, 1, 0, 4)
    large(7, 1, 1)
    large(7, 1, 0)
    final_small(keeps_high, 3, 1, 0, 4)
    final_large(keeps_high, 3, 1)
    final_small(keeps_low, 0, 4, 2, 2)

    def show(block):
        out_ref[:, pl.ds(pl.multiple_of(block * 128, 128), 128)] = obuf[block]

    @pl.loop(0, 4)
    def _(kk):
        show(block_of(kk, z % 2, c))
        o_copy(kk).wait_recv()
        show(block_of(kk, z % 2, 1 - c))
        for other in range(2):
            for j in range(CHUNKS):
                op_copy(kk, j, other).wait_recv()
            show(block_of(kk, 1 - z % 2, c if other == 0 else 1 - c))
        for t in range(2):
            p_copy(kk, t).wait_send()
        o_copy(kk).wait_send()
        for j in range(CHUNKS):
            q_copy(kk, j).wait_send()
            for other in range(2):
                op_copy(kk, j, other).wait_send()

    @pl.loop(0, HALF)
    def _(g):
        sb_copy(g).wait_send()
        sp_copy(g).wait_send()

    @pl.loop(0, OWN)
    def _(i):
        x_copy(i).wait_send()
        xp_copy(i).wait_send()

        @pl.when(has_up)
        def _():
            z_copy(i).wait_send()
    for j in range(CHUNKS):
        att_z(j).wait_send()
        att_fwd(j).wait_send()
    att_sib.wait_send()
    for q in range(WQ):
        for slot in range(1, 4):
            w_out(slot, q).wait_send()


def fused(queries, keys, values, features, weight):
    tok, columns = queries.shape
    heads = features.shape[0]
    depth = weight.shape[0]
    f32, bf16 = jnp.float32, jnp.bfloat16
    vmem = pltpu.VMEM
    dma = pltpu.SemaphoreType.DMA
    rows = DH + TAIL
    part = tok // CHUNKS
    return pl.pallas_call(
        kernel_body,
        out_shape=jax.ShapeDtypeStruct((tok, columns), bf16),
        in_specs=[pl.BlockSpec(memory_space=pl.ANY)] * 5,
        out_specs=pl.BlockSpec(memory_space=pltpu.VMEM),
        scratch_shapes=[
            vmem((tok, columns), bf16),
            vmem((tok, columns), bf16),
            vmem((tok, columns), bf16),
            vmem(features.shape, f32),
            vmem((8, depth, 128), bf16),
            vmem((heads, 2 * DH, M), bf16),
            vmem((heads, tok, M), bf16),
            vmem((heads, tok, M), bf16),
            vmem((heads, rows, tok), bf16),
            vmem((heads, tok, rows), f32),
            vmem((HALF, rows, M), f32),
            vmem((HALF, rows, M), f32),
            vmem((HALF, rows, M), f32),
            vmem((OWN, rows, M), bf16),
            vmem((OWN, rows, M), bf16),
            vmem((OWN, rows, M), bf16),
            vmem((OWN, rows, M), bf16),
            vmem((OWN, rows, M), bf16),
            vmem((OWN, rows, M), bf16),
            vmem((heads, rows, M), f32),
            vmem((HALF, rows, M), f32),
            vmem((2, tok, columns), bf16),
            vmem((CHUNKS, 2 * part, columns), bf16),
            vmem((4, 2, tok, 128), f32),
            vmem((4, CHUNKS, 2 * part, 128), f32),
            vmem((4, 2, tok, 128), bf16),
            vmem((4, 2, tok, 128), bf16),
            vmem((4, CHUNKS, 2 * part, 128), bf16),
            vmem((4, CHUNKS, 2 * part, 128), bf16),
            vmem((4, tok, 128), bf16),
            vmem((4, CHUNKS, 2 * part, 128), bf16),
            vmem((16, tok, 128), bf16),
            dma((4,)), dma((WQ,)), dma((3, WQ)), dma((3, WQ)), dma((HALF,)), dma((HALF,)),
            dma((OWN,)), dma((OWN,)), dma((OWN,)), dma((OWN,)), dma((OWN,)), dma((OWN,)),
            dma((HALF,)), dma((HALF,)), dma((2 * CHUNKS + 1,)), dma((2 * CHUNKS + 1,)),
            dma((4, 2)), dma((4, 2)), dma((4, CHUNKS)), dma((4, CHUNKS)),
            dma((4,)), dma((4,)), dma((4, CHUNKS, 2)), dma((4, CHUNKS, 2)),
        ],
        compiler_params=pltpu.CompilerParams(
            collective_id=0, has_side_effects=True, vmem_limit_bytes=60 << 20),
    )(queries, keys, values, features, weight)


def shards(queries, keys, values, features, output_proj_weight):
    fits = (
        lax.axis_size("seq") == PLANE * DEPTH
        and lax.axis_size("head") == 2
        and features.shape == (2 * HALF, DH, M)
        and queries.shape == (256, 2048)
        and output_proj_weight.shape == (2048, 256)
    )
    step = fused if fits else plain
    return step(queries, keys, values, features, output_proj_weight)


def solution(mesh):
    in_specs = (
        P("seq", "head"),
        P("seq", "head"),
        P("seq", "head"),
        P("head", None, None),
        P("head", "seq"),
    )
    return jax.shard_map(
        shards, mesh=mesh, in_specs=in_specs, out_specs=P("seq", "head"), check_vma=False
    )
```

```python
import math

import jax
import jax.numpy as jnp
from jax import lax
from jax.experimental import pallas as pl
from jax.experimental.pallas import tpu as pltpu
from jax.sharding import PartitionSpec as P

DH = 128
M = 256
HIGH = lax.Precision.HIGHEST


def feature_map(x, direction):
    x = x * DH ** (-0.25)
    proj = jnp.einsum("htd,hdm->htm", x, direction, precision=HIGH)
    return jnp.exp(proj - 0.5 * jnp.sum(x * x, axis=-1, keepdims=True)) / math.sqrt(M)


def plain(queries, keys, values, features, output_proj_weight):
    tok_rows = queries.shape[0]
    local_heads = features.shape[0]
    devices, here = lax.axis_size("seq"), lax.axis_index("seq")
    halves, half = lax.axis_size("head"), lax.axis_index("head")

    def split_heads(arr):
        return arr.astype(jnp.float32).reshape(tok_rows, local_heads, DH).transpose(1, 0, 2)

    kf = feature_map(split_heads(keys), features)
    v = split_heads(values)
    v = jnp.concatenate([v, jnp.ones((local_heads, tok_rows, 8), jnp.float32)], axis=2)
    state = jnp.einsum("htp,htk->hpk", v, kf, precision=HIGH)
    states = lax.all_gather(state.astype(jnp.bfloat16), "seq")
    state, weight = lax.optimization_barrier((state, output_proj_weight))
    whole = lax.all_gather(weight, "seq", axis=1, tiled=True)
    qf = feature_map(split_heads(queries), features)
    lower = jnp.tril(jnp.ones((tok_rows, tok_rows), jnp.float32))
    scores = jnp.einsum("htm,hsm->hts", qf, kf, precision=HIGH) * lower
    both = jnp.einsum("hts,hsd->htd", scores, v, precision=HIGH)
    earlier = (jnp.arange(devices) < here)[:, None, None, None]
    prior = jnp.sum(jnp.where(earlier, states.astype(jnp.float32), 0.0), axis=0)
    both = both + jnp.einsum("htk,hpk->htp", qf, prior, precision=HIGH)
    attended = both[:, :, :DH] / both[:, :, DH : DH + 1]
    attended = attended.transpose(1, 0, 2).reshape(tok_rows, local_heads * DH).astype(jnp.bfloat16)
    partial = jnp.dot(attended, whole, preferred_element_type=jnp.float32)
    width = partial.shape[1] // halves
    total = lax.dynamic_slice_in_dim(partial, half * width, width, 1)
    for shift in range(1, halves):
        theirs = lax.rem(half + shift, halves)
        piece = lax.dynamic_slice_in_dim(partial, theirs * width, width, 1).astype(jnp.bfloat16)
        got = lax.ppermute(piece, "head", [(i, (i + shift) % halves) for i in range(halves)])
        total = total + got.astype(jnp.float32)
    return total.astype(jnp.bfloat16)


PLANE, DEPTH = 4, 4
HALF = 8
OWN = 4
TAIL = 16
WQ = 8
CHUNKS = 4
UNROLL = 4
LOG2E = math.log2(math.e)


def kernel_body(q_hbm, k_hbm, v_hbm, f_hbm, w_hbm, out_ref, q_ref, k_ref, v_ref, f_ref, wbuf, fhl,
                kf, qf, vt, both, own32, sibst, sbsend, xsend, xrecv, below, back, xpsend, xprior,
                prior, sbp, attb, attp, acc, accp, psend, precv, qsend, qrecv, osend, opsend, obuf,
                in_sem, w_load, w_send, w_recv, sb_send, sb_recv, x_send, x_recv, z_send, z_recv,
                xp_send, xp_recv, sp_send, sp_recv, at_send, at_recv, p_send, p_recv,
                pp_send, pp_recv, o_send, o_recv, op_send, op_recv, show_sem,
                passed):
    f32, bf16 = jnp.float32, jnp.bfloat16
    tok = q_ref.shape[0]
    ctok = tok // CHUNKS
    heads = f_ref.shape[0]
    qrows = w_hbm.shape[0] // 4
    me, y = lax.axis_index("seq"), lax.axis_index("head")
    z, x, c = me // PLANE, (me // 2) % 2, me % 2
    sib, xn, up, down = me + 1 - 2 * c, me + 2 - 4 * x, me + PLANE, me - PLANE
    pz = me + PLANE - 2 * PLANE * (z % 2)
    pzsib = pz + 1 - 2 * c
    far = me + 2 * PLANE - 4 * PLANE * (z // 2)
    has_up, has_down = z < DEPTH - 1, z > 0

    loads = [pltpu.make_async_copy(a, b, in_sem.at[i]) for i, (a, b) in enumerate(
        ((k_hbm, k_ref), (f_hbm, f_ref), (v_hbm, v_ref), (q_hbm, q_ref)))]
    for one in loads:
        one.start()
    barrier = pltpu.get_barrier_semaphore()

    def greet(device):
        pl.semaphore_signal(barrier, inc=1, device_id=device, device_id_type=pl.DeviceIdType.MESH)

    for device in ((sib, y), (xn, y), (me, 1 - y), (far, y), (pzsib, y)):
        greet(device)

    @pl.when(has_up)
    def _():
        greet((up, y))

    @pl.when(has_down)
    def _():
        greet((down, y))

    pl.semaphore_wait(barrier, 5 + has_up.astype(jnp.int32) + has_down.astype(jnp.int32))

    def remote(src, dst, ssem, rsem, device):
        return pltpu.make_async_remote_copy(
            src_ref=src, dst_ref=dst, send_sem=ssem, recv_sem=rsem, device_id=(device, y),
            device_id_type=pl.DeviceIdType.MESH)

    def place(slot, q):
        return wbuf.at[2 * slot + q // 4, pl.ds((q % 4) * qrows, qrows)]

    def origin(q):
        return w_hbm.at[pl.ds((q % 4) * qrows, qrows), pl.ds((q // 4) * 128, 128)]

    def w_out(slot, q):
        src = origin(q) if slot < 3 else place(2, q)
        return remote(src, place(slot, q), w_send.at[slot - 1, q], w_recv.at[slot - 1, q],
                      far if slot == 2 else xn)

    def w_wait(slot, *qs):
        for q in qs:
            w_out(slot, q).wait_recv()

    def w_go(slot, cond, *qs):
        def start():
            for q in qs:
                w_out(slot, q).start()
        if cond is None:
            start()
        else:
            pl.when(cond)(start)

    def forward(*qs):
        for q in qs:
            w_out(2, q).wait_recv()
            w_out(3, q).start()

    own_loads = [pltpu.make_async_copy(origin(q), place(0, q), w_load.at[q]) for q in range(WQ)]
    w_go(2, z == 0, 0, 1)
    w_go(1, z == 1, 0)
    w_go(2, z == 1, 0, 1)
    w_go(1, z == 2, 0)
    w_go(2, z == 2, 0, 1, 2, 3, 4, 5)
    w_go(2, z == 3, 0, 1, 2, 3, 4)

    scale = DH ** (-0.25)

    def cols(h):
        return pl.ds(pl.multiple_of(h * DH, DH), DH)

    def feature_map(t, split):
        tf = t.astype(f32)
        norm = jnp.sum(tf * tf, axis=-1, keepdims=True) * (0.5 * scale * scale * LOG2E)
        proj = jnp.dot(jnp.concatenate([t, t], axis=1), split, preferred_element_type=f32)
        return jnp.exp2(proj - (norm + 0.5 * math.log2(M))).astype(bf16)

    hi_row = lax.broadcasted_iota(jnp.int32, (TAIL, M), 0) < TAIL // 2

    def narrow(s):
        tail = s[DH:]
        tail = tail + pltpu.roll(tail, TAIL // 2, 0)
        hi = tail.astype(bf16).astype(f32)
        tail = jnp.where(hi_row, hi, tail - hi)
        return jnp.concatenate([s[:DH].astype(bf16), tail.astype(bf16)], axis=0)

    def key_state(h):
        f = f_ref[h] * (scale * LOG2E)
        hi = f.astype(bf16)
        split = jnp.concatenate([hi, (f - hi.astype(f32)).astype(bf16)], axis=0)
        fhl[h] = split
        feats = feature_map(k_ref[:, cols(h)], split)
        kf[h] = feats
        flipped = jnp.concatenate([v_ref[:, cols(h)].T, jnp.ones((TAIL, tok), bf16)], axis=0)
        vt[h] = flipped
        s = jnp.dot(flipped, feats, preferred_element_type=f32)
        return jnp.concatenate([s[:DH], jnp.where(hi_row, s[DH:], 0.0)], axis=0)

    def sb_copy(g):
        return remote(sbsend.at[g], sibst.at[g], sb_send.at[g], sb_recv.at[g], sib)

    def x_copy(i):
        return remote(xsend.at[i], xrecv.at[i], x_send.at[i], x_recv.at[i], xn)

    for one in loads[:3]:
        one.wait()

    @pl.loop(0, OWN + 1)
    def _(i):
        @pl.when(i < OWN)
        def _():
            for g in (OWN * (1 - x) + i, OWN * x + i):
                sbsend[g] = key_state(HALF * (1 - c) + g)
                sb_copy(g).start()
                own32[g] = key_state(HALF * c + g)

        @pl.when(i > 0)
        def _():
            g = OWN * (1 - x) + i - 1
            sb_copy(g).wait_recv()
            sb_copy(OWN * x + i - 1).wait_recv()
            xsend[i - 1] = narrow(own32[g] + sibst[g])
            x_copy(i - 1).start()

    w_go(1, z == 0, 0)
    w_go(1, z == 1, 1)
    w_go(2, z == 1, 2)
    w_go(1, z == 2, 1, 2)
    w_go(1, z == 3, 0, 1, 2)
    for one in own_loads:
        one.start()
    loads[3].wait()
    lower = (lax.broadcasted_iota(jnp.int32, (tok, tok), 1)
             <= lax.broadcasted_iota(jnp.int32, (tok, tok), 0))

    def across(a, b):
        return lax.dot_general(a, b, (((1,), (1,)), ((), ())), preferred_element_type=f32)

    def local_heads(start, stop):
        @pl.loop(start, stop)
        def _(i):
            some = [UNROLL * i + j for j in range(UNROLL)]
            qs = [feature_map(q_ref[:, cols(h)], fhl[h]) for h in some]
            scores = [jnp.where(lower, across(qh, kf[h]), 0.0).astype(bf16)
                      for h, qh in zip(some, qs)]
            sums = [across(s, vt[h]) for h, s in zip(some, scores)]
            for h, qh, total in zip(some, qs, sums):
                qf[h] = qh
                both[h] = total

    steps = heads // UNROLL
    before = jnp.where(z == 0, 0, steps)
    local_heads(0, before)

    at_x0, at_x1 = (x == 0).astype(f32), (x == 1).astype(f32)
    at_c0, at_c1 = (c == 0).astype(f32), (c == 1).astype(f32)

    def sp_copy(g):
        return remote(sbp.at[g], prior.at[HALF * c + g], sp_send.at[g], sp_recv.at[g], sib)

    def put_priors(g, base):
        sbp[g] = base + at_c0 * own32[g]
        sp_copy(g).start()
        prior[HALF * c + g] = base + at_c1 * sibst[g]

    def z_copy(i):
        return remote(back.at[i], below.at[i], z_send.at[i], z_recv.at[i], up)

    def xp_copy(i):
        return remote(xpsend.at[i], xprior.at[i], xp_send.at[i], xp_recv.at[i], xn)

    @pl.loop(0, OWN)
    def _(i):
        g = OWN * x + i
        x_copy(i).wait_recv()

        @pl.when(has_down)
        def _():
            z_copy(i).wait_recv()

        @pl.when(z == 0)
        def _():
            below[i] = jnp.zeros(below.shape[1:], bf16)

        chip = own32[g] + sibst[g]
        under = below[i].astype(f32)
        theirs = xrecv[i].astype(f32)

        @pl.when(has_up)
        def _():
            back[i] = narrow(under + chip + theirs)
            z_copy(i).start()
        xpsend[i] = narrow(under + at_x0 * chip)
        xp_copy(i).start()
        put_priors(g, under + at_x1 * theirs)

    @pl.when(z >= 2)
    def _():
        pl.semaphore_signal(passed, inc=1, device_id=(far, y),
                            device_id_type=pl.DeviceIdType.MESH)

    w_go(1, z == 0, 1, 2, 3, 4, 5)
    w_go(1, z == 1, 2, 3, 4, 5)
    w_go(1, z == 2, 3, 4, 5)
    w_go(2, z == 2, 6, 7)
    w_go(1, z == 3, 3, 4, 5)
    w_go(2, z == 3, 5, 6, 7)
    local_heads(before, steps)

    def finish(some):
        done = []
        for h in some:
            p = prior[h]
            hi = p.astype(bf16)
            lo = (p - hi.astype(f32)).astype(bf16)
            old = across(jnp.concatenate([qf[h], qf[h]], axis=1),
                         jnp.concatenate([hi, lo], axis=1))
            here, at = both[h], DH + TAIL // 2
            den = here[:, DH : DH + 1] + old[:, DH : DH + 1] + old[:, at : at + 1]
            done.append(((here[:, :DH] + old[:, :DH]) * (1.0 / den)).astype(bf16))
        for h, part in zip(some, done):
            attb[0, :, cols(h)] = part

    def finish_group(first):
        finish([HALF * c + first + i for i in range(OWN)])

        @pl.loop(first, first + OWN)
        def _(g):
            remote(sbp.at[g], prior.at[HALF * (1 - c) + g], sp_send.at[g], sp_recv.at[g],
                   sib).wait_recv()
        finish([HALF * (1 - c) + first + i for i in range(OWN)])

    finish_group(OWN * x)

    @pl.loop(0, OWN)
    def _(i):
        xp_copy(i).wait_recv()
        put_priors(OWN * (1 - x) + i, xprior[i].astype(f32))

    finish_group(OWN * (1 - x))

    def resume():
        pl.semaphore_wait(passed, 1)

    def att_z(j):
        return remote(attb.at[0, pl.ds(j * ctok, ctok)], attp.at[j, pl.ds(0, ctok)],
                      at_send.at[j], at_recv.at[j], pz)

    def att_fwd(j):
        return remote(attp.at[j, pl.ds(0, ctok)], attp.at[j, pl.ds(ctok, ctok)],
                      at_send.at[CHUNKS + j], at_recv.at[CHUNKS + j], sib)

    att_sib = remote(attb.at[0], attb.at[1], at_send.at[2 * CHUNKS], at_recv.at[2 * CHUNKS], sib)
    pl.when(z == 0)(resume)
    w_go(2, z == 0, 2)
    att_z(0).start()
    w_go(2, z == 0, 3, 4)
    att_z(1).start()
    w_go(2, z == 0, 5)
    att_z(2).start()
    w_go(2, z == 0, 6, 7)
    att_z(3).start()
    att_sib.start()

    keeps_low = y == z // 2
    keeps_high = jnp.logical_not(keeps_low)

    def p_copy(kk, t):
        return pltpu.make_async_remote_copy(
            src_ref=psend.at[kk, t], dst_ref=precv.at[kk, t], send_sem=p_send.at[kk, t],
            recv_sem=p_recv.at[kk, t], device_id=(me, 1 - y), device_id_type=pl.DeviceIdType.MESH)

    def q_copy(kk, j):
        return pltpu.make_async_remote_copy(
            src_ref=qsend.at[kk, j], dst_ref=qrecv.at[kk, j], send_sem=pp_send.at[kk, j],
            recv_sem=pp_recv.at[kk, j], device_id=(me, 1 - y), device_id_type=pl.DeviceIdType.MESH)

    def item(src, hh, t, sums, out, copy):
        piece = jnp.dot(src[t], wbuf[hh], preferred_element_type=f32)
        kk = hh % 4
        keep = (hh // 4 == 0) == keeps_low

        @pl.when(keep)
        def _():
            sums[kk, t] = piece

        @pl.when(jnp.logical_not(keep))
        def _():
            out[kk, t] = piece.astype(bf16)
            copy(kk, t).start()

    def pair(src, slot, t, sums, out, copy):
        weight = jnp.concatenate([wbuf[2 * slot], wbuf[2 * slot + 1]], axis=1)
        piece = jnp.dot(src[t], weight, preferred_element_type=f32)
        first = 2 * (slot % 2)
        keep = (slot // 2 == 0) == keeps_low

        @pl.when(keep)
        def _():
            sums[first, t] = piece[:, :128]
            sums[first + 1, t] = piece[:, 128:]

        @pl.when(jnp.logical_not(keep))
        def _():
            for i in range(2):
                out[first + i, t] = piece[:, 128 * i : 128 * (i + 1)].astype(bf16)
                copy(first + i, t).start()

    def large_pair(slot):
        @pl.loop(0, 2)
        def _(t):
            pair(attb, slot, t, acc, psend, p_copy)

    def small_pair(slot, first_j, many=1):
        @pl.loop(first_j, first_j + many)
        def _(j):
            pair(attp, slot, j, accp, qsend, q_copy)

    def large(first_hh, count, t):
        @pl.loop(first_hh, first_hh + count)
        def _(hh):
            item(attb, hh, t, acc, psend, p_copy)

    def small(first_hh, count, first_j, many=1):
        @pl.loop(0, count * many)
        def _(i):
            item(attp, first_hh + i % count, first_j + i // count, accp, qsend, q_copy)

    def block_of(kk, zz, cc):
        xs = jnp.where(kk // 2 == 0, x, 1 - x)
        return ((zz * 2 + xs) * 2 + cc) * 2 + kk % 2

    def o_copy(kk):
        return remote(osend.at[kk], obuf.at[block_of(kk, z % 2, c)], o_send.at[kk], o_recv.at[kk],
                      sib)

    def op_copy(kk, j, other):
        return remote(opsend.at[kk, j, pl.ds(other * ctok, ctok)],
                      obuf.at[block_of(kk, z % 2, c), pl.ds(j * ctok, ctok)],
                      op_send.at[kk, j, other], op_recv.at[kk, j, other], (pz, pzsib)[other])

    def final_large(cond, first_kk, count):
        @pl.when(cond)
        def _():
            @pl.loop(first_kk, first_kk + count)
            def _(kk):
                p_copy(kk, 1).wait_recv()
                osend[kk] = (acc[kk, 1] + precv[kk, 1].astype(f32)).astype(bf16)
                o_copy(kk).start()
                p_copy(kk, 0).wait_recv()
                obuf[block_of(kk, z % 2, c)] = (acc[kk, 0] + precv[kk, 0].astype(f32)).astype(bf16)

    def final_small(cond, first_kk, count, first_j, many=1):
        @pl.when(cond)
        def _():
            @pl.loop(0, count * many)
            def _(i):
                kk, j = first_kk + i % count, first_j + i // count
                q_copy(kk, j).wait_recv()
                opsend[kk, j] = (accp[kk, j] + qrecv[kk, j].astype(f32)).astype(bf16)
                op_copy(kk, j, 0).start()
                op_copy(kk, j, 1).start()

    def take(j):
        att_z(j).wait_recv()
        att_fwd(j).start()

    def at_planes(cond, takes, forwards):
        @pl.when(cond)
        def _():
            for j in takes:
                take(j)
            forward(*forwards)

    w_go(1, None, 6, 7)
    for one in own_loads:
        one.wait()
    att_sib.wait_recv()
    large_pair(0)
    pl.when(z == 1)(resume)
    w_go(2, z == 1, 3, 4, 5, 6, 7)
    at_planes((z == 0) | (z == 1) | (z == 2), (), (4, ))
    forward(0, 1, 2, 3)
    large(4, 1, 0)
    large(4, 1, 1)
    take(0)
    take(1)
    at_planes((z == 3), (), (4, ))
    att_fwd(0).wait_recv()
    att_fwd(1).wait_recv()
    small_pair(0, 0, 2)
    at_planes((z == 1), (), (5, ))
    w_wait(1, 0, 1, 2, 3, 4, 5, 6, 7)
    large_pair(1)
    at_planes((z == 0) | (z == 2), (), (5, ))
    at_planes((z == 2), (), (6, ))
    w_wait(3, 0, 1, 2, 3)
    large(6, 1, 0)
    large(6, 1, 1)
    at_planes((z == 3), (), (5, ))
    small(4, 1, 0, 2)
    at_planes((z == 1), (), (6, 7, ))
    small(6, 1, 0, 2)
    at_planes((z == 0) | (z == 2) | (z == 3), (), (7, ))
    at_planes((z == 0) | (z == 3), (), (6, ))
    large(5, 1, 0)
    large(5, 1, 1)
    small(5, 1, 0, 2)
    small_pair(1, 0, 2)
    take(2)
    take(3)
    att_fwd(2).wait_recv()
    att_fwd(3).wait_recv()
    small_pair(1, 2, 2)
    final_large(keeps_low, 0, 4)
    final_small(keeps_low, 0, 4, 0, 2)
    final_large(keeps_high, 0, 1)
    final_small(keeps_high, 0, 1, 0, 2)
    small(4, 3, 2, 2)
    final_large(keeps_high, 1, 1)
    final_small(keeps_high, 1, 1, 0, 2)
    small_pair(0, 2, 2)
    final_large(keeps_high, 2, 1)
    final_small(keeps_high, 2, 1, 0, 2)
    final_small(keeps_high, 0, 3, 2, 2)
    w_wait(3, 4, 5, 6, 7)
    small(7, 1, 0, 4)
    large(7, 1, 1)
    large(7, 1, 0)
    final_small(keeps_low, 0, 4, 2, 2)
    final_small(keeps_high, 3, 1, 0, 4)
    final_large(keeps_high, 3, 1)

    def show(block):
        shown(block).start()

    def shown(block):
        return pltpu.make_async_copy(
            obuf.at[block], out_ref.at[:, pl.ds(pl.multiple_of(block * 128, 128), 128)],
            show_sem.at[block])

    @pl.loop(0, 4)
    def _(kk):
        show(block_of(kk, z % 2, c))
        o_copy(kk).wait_recv()
        show(block_of(kk, z % 2, 1 - c))
        for other in range(2):
            for j in range(CHUNKS):
                op_copy(kk, j, other).wait_recv()
            show(block_of(kk, 1 - z % 2, c if other == 0 else 1 - c))
        for t in range(2):
            p_copy(kk, t).wait_send()
        o_copy(kk).wait_send()
        for j in range(CHUNKS):
            q_copy(kk, j).wait_send()
            for other in range(2):
                op_copy(kk, j, other).wait_send()

    @pl.loop(0, HALF)
    def _(g):
        sb_copy(g).wait_send()
        sp_copy(g).wait_send()

    @pl.loop(0, OWN)
    def _(i):
        x_copy(i).wait_send()
        xp_copy(i).wait_send()

        @pl.when(has_up)
        def _():
            z_copy(i).wait_send()
    for j in range(CHUNKS):
        att_z(j).wait_send()
        att_fwd(j).wait_send()
    att_sib.wait_send()
    for q in range(WQ):
        for slot in range(1, 4):
            w_out(slot, q).wait_send()

    @pl.loop(0, 16)
    def _(block):
        shown(block).wait()


def fused(queries, keys, values, features, weight):
    tok, columns = queries.shape
    heads = features.shape[0]
    depth = weight.shape[0]
    f32, bf16 = jnp.float32, jnp.bfloat16
    vmem = pltpu.VMEM
    dma = pltpu.SemaphoreType.DMA
    rows = DH + TAIL
    part = tok // CHUNKS
    return pl.pallas_call(
        kernel_body,
        out_shape=jax.ShapeDtypeStruct((tok, columns), bf16),
        in_specs=[pl.BlockSpec(memory_space=pl.ANY)] * 5,
        out_specs=pl.BlockSpec(memory_space=pl.ANY),
        scratch_shapes=[
            vmem((tok, columns), bf16),
            vmem((tok, columns), bf16),
            vmem((tok, columns), bf16),
            vmem(features.shape, f32),
            vmem((8, depth, 128), bf16),
            vmem((heads, 2 * DH, M), bf16),
            vmem((heads, tok, M), bf16),
            vmem((heads, tok, M), bf16),
            vmem((heads, rows, tok), bf16),
            vmem((heads, tok, rows), f32),
            vmem((HALF, rows, M), f32),
            vmem((HALF, rows, M), f32),
            vmem((HALF, rows, M), f32),
            vmem((OWN, rows, M), bf16),
            vmem((OWN, rows, M), bf16),
            vmem((OWN, rows, M), bf16),
            vmem((OWN, rows, M), bf16),
            vmem((OWN, rows, M), bf16),
            vmem((OWN, rows, M), bf16),
            vmem((heads, rows, M), f32),
            vmem((HALF, rows, M), f32),
            vmem((2, tok, columns), bf16),
            vmem((CHUNKS, 2 * part, columns), bf16),
            vmem((4, 2, tok, 128), f32),
            vmem((4, CHUNKS, 2 * part, 128), f32),
            vmem((4, 2, tok, 128), bf16),
            vmem((4, 2, tok, 128), bf16),
            vmem((4, CHUNKS, 2 * part, 128), bf16),
            vmem((4, CHUNKS, 2 * part, 128), bf16),
            vmem((4, tok, 128), bf16),
            vmem((4, CHUNKS, 2 * part, 128), bf16),
            vmem((16, tok, 128), bf16),
            dma((4,)), dma((WQ,)), dma((3, WQ)), dma((3, WQ)), dma((HALF,)), dma((HALF,)),
            dma((OWN,)), dma((OWN,)), dma((OWN,)), dma((OWN,)), dma((OWN,)), dma((OWN,)),
            dma((HALF,)), dma((HALF,)), dma((2 * CHUNKS + 1,)), dma((2 * CHUNKS + 1,)),
            dma((4, 2)), dma((4, 2)), dma((4, CHUNKS)), dma((4, CHUNKS)),
            dma((4,)), dma((4,)), dma((4, CHUNKS, 2)), dma((4, CHUNKS, 2)),
            dma((16,)), pltpu.SemaphoreType.REGULAR,
        ],
        compiler_params=pltpu.CompilerParams(
            collective_id=0, has_side_effects=True, vmem_limit_bytes=60 << 20),
    )(queries, keys, values, features, weight)


def shards(queries, keys, values, features, output_proj_weight):
    fits = (
        lax.axis_size("seq") == PLANE * DEPTH
        and lax.axis_size("head") == 2
        and features.shape == (2 * HALF, DH, M)
        and queries.shape == (256, 2048)
        and output_proj_weight.shape == (2048, 256)
    )
    step = fused if fits else plain
    return step(queries, keys, values, features, output_proj_weight)


def solution(mesh):
    in_specs = (
        P("seq", "head"),
        P("seq", "head"),
        P("seq", "head"),
        P("head", None, None),
        P("head", "seq"),
    )
    return jax.shard_map(
        shards, mesh=mesh, in_specs=in_specs, out_specs=P("seq", "head"), check_vma=False
    )
```

```python
import math

import jax
import jax.numpy as jnp
from jax import lax
from jax.experimental import pallas as pl
from jax.experimental.pallas import tpu as pltpu
from jax.sharding import PartitionSpec as P

DH = 128
M = 256
HIGH = lax.Precision.HIGHEST


def feature_map(x, direction):
    x = x * DH ** (-0.25)
    proj = jnp.einsum("htd,hdm->htm", x, direction, precision=HIGH)
    return jnp.exp(proj - 0.5 * jnp.sum(x * x, axis=-1, keepdims=True)) / math.sqrt(M)


def plain(queries, keys, values, features, output_proj_weight):
    tok_rows = queries.shape[0]
    local_heads = features.shape[0]
    devices, here = lax.axis_size("seq"), lax.axis_index("seq")
    halves, half = lax.axis_size("head"), lax.axis_index("head")

    def split_heads(arr):
        return arr.astype(jnp.float32).reshape(tok_rows, local_heads, DH).transpose(1, 0, 2)

    kf = feature_map(split_heads(keys), features)
    v = split_heads(values)
    v = jnp.concatenate([v, jnp.ones((local_heads, tok_rows, 8), jnp.float32)], axis=2)
    state = jnp.einsum("htp,htk->hpk", v, kf, precision=HIGH)
    states = lax.all_gather(state.astype(jnp.bfloat16), "seq")
    state, weight = lax.optimization_barrier((state, output_proj_weight))
    whole = lax.all_gather(weight, "seq", axis=1, tiled=True)
    qf = feature_map(split_heads(queries), features)
    lower = jnp.tril(jnp.ones((tok_rows, tok_rows), jnp.float32))
    scores = jnp.einsum("htm,hsm->hts", qf, kf, precision=HIGH) * lower
    both = jnp.einsum("hts,hsd->htd", scores, v, precision=HIGH)
    earlier = (jnp.arange(devices) < here)[:, None, None, None]
    prior = jnp.sum(jnp.where(earlier, states.astype(jnp.float32), 0.0), axis=0)
    both = both + jnp.einsum("htk,hpk->htp", qf, prior, precision=HIGH)
    attended = both[:, :, :DH] / both[:, :, DH : DH + 1]
    attended = attended.transpose(1, 0, 2).reshape(tok_rows, local_heads * DH).astype(jnp.bfloat16)
    partial = jnp.dot(attended, whole, preferred_element_type=jnp.float32)
    width = partial.shape[1] // halves
    total = lax.dynamic_slice_in_dim(partial, half * width, width, 1)
    for shift in range(1, halves):
        theirs = lax.rem(half + shift, halves)
        piece = lax.dynamic_slice_in_dim(partial, theirs * width, width, 1).astype(jnp.bfloat16)
        got = lax.ppermute(piece, "head", [(i, (i + shift) % halves) for i in range(halves)])
        total = total + got.astype(jnp.float32)
    return total.astype(jnp.bfloat16)


PLANE, DEPTH = 4, 4
HALF = 8
OWN = 4
TAIL = 16
WQ = 8
CHUNKS = 4
UNROLL = 4
LOG2E = math.log2(math.e)


def kernel_body(q_hbm, k_hbm, v_hbm, f_hbm, w_hbm, out_ref, q_ref, k_ref, v_ref, f_ref, wbuf, fhl,
                kf, qf, vt, both, own32, sibst, sbsend, xsend, xrecv, below, back, xpsend, xprior,
                prior, sbp, attb, attp, acc, accp, psend, precv, qsend, qrecv, osend, opsend, obuf,
                in_sem, w_load, w_send, w_recv, sb_send, sb_recv, x_send, x_recv, z_send, z_recv,
                xp_send, xp_recv, sp_send, sp_recv, at_send, at_recv, p_send, p_recv,
                pp_send, pp_recv, o_send, o_recv, op_send, op_recv, show_sem,
                passed):
    f32, bf16 = jnp.float32, jnp.bfloat16
    tok = q_ref.shape[0]
    ctok = tok // CHUNKS
    heads = f_ref.shape[0]
    qrows = w_hbm.shape[0] // 4
    me, y = lax.axis_index("seq"), lax.axis_index("head")
    z, x, c = me // PLANE, (me // 2) % 2, me % 2
    sib, xn, up, down = me + 1 - 2 * c, me + 2 - 4 * x, me + PLANE, me - PLANE
    pz = me + PLANE - 2 * PLANE * (z % 2)
    pzsib = pz + 1 - 2 * c
    far = me + 2 * PLANE - 4 * PLANE * (z // 2)
    has_up, has_down = z < DEPTH - 1, z > 0

    loads = [pltpu.make_async_copy(a, b, in_sem.at[i]) for i, (a, b) in enumerate(
        ((k_hbm, k_ref), (f_hbm, f_ref), (v_hbm, v_ref), (q_hbm, q_ref)))]
    for one in loads:
        one.start()
    barrier = pltpu.get_barrier_semaphore()

    def greet(device):
        pl.semaphore_signal(barrier, inc=1, device_id=device, device_id_type=pl.DeviceIdType.MESH)

    for device in ((sib, y), (xn, y), (me, 1 - y), (far, y), (pzsib, y)):
        greet(device)

    @pl.when(has_up)
    def _():
        greet((up, y))

    @pl.when(has_down)
    def _():
        greet((down, y))

    pl.semaphore_wait(barrier, 5 + has_up.astype(jnp.int32) + has_down.astype(jnp.int32))

    def remote(src, dst, ssem, rsem, device):
        return pltpu.make_async_remote_copy(
            src_ref=src, dst_ref=dst, send_sem=ssem, recv_sem=rsem, device_id=(device, y),
            device_id_type=pl.DeviceIdType.MESH)

    def place(slot, q):
        return wbuf.at[2 * slot + q // 4, pl.ds((q % 4) * qrows, qrows)]

    def origin(q):
        return w_hbm.at[pl.ds((q % 4) * qrows, qrows), pl.ds((q // 4) * 128, 128)]

    def w_out(slot, q):
        src = origin(q) if slot < 3 else place(2, q)
        return remote(src, place(slot, q), w_send.at[slot - 1, q], w_recv.at[slot - 1, q],
                      far if slot == 2 else xn)

    def w_wait(slot, *qs):
        for q in qs:
            w_out(slot, q).wait_recv()

    def w_go(slot, cond, *qs):
        def start():
            for q in qs:
                w_out(slot, q).start()
        if cond is None:
            start()
        else:
            pl.when(cond)(start)

    def forward(*qs):
        for q in qs:
            w_out(2, q).wait_recv()
            w_out(3, q).start()

    own_loads = [pltpu.make_async_copy(origin(q), place(0, q), w_load.at[q]) for q in range(WQ)]
    w_go(2, z == 0, 0, 1)
    w_go(1, z == 1, 0)
    w_go(2, z == 1, 0, 1)
    w_go(1, z == 2, 0)
    w_go(2, z == 2, 0, 1, 2, 3, 4, 5, 6, 7)
    w_go(2, z == 3, 0, 1, 2, 3)

    scale = DH ** (-0.25)

    def cols(h):
        return pl.ds(pl.multiple_of(h * DH, DH), DH)

    def feature_map(t, split):
        tf = t.astype(f32)
        norm = jnp.sum(tf * tf, axis=-1, keepdims=True) * (0.5 * scale * scale * LOG2E)
        proj = jnp.dot(jnp.concatenate([t, t], axis=1), split, preferred_element_type=f32)
        return jnp.exp2(proj - (norm + 0.5 * math.log2(M))).astype(bf16)

    hi_row = lax.broadcasted_iota(jnp.int32, (TAIL, M), 0) < TAIL // 2

    def narrow(s):
        tail = s[DH:]
        tail = tail + pltpu.roll(tail, TAIL // 2, 0)
        hi = tail.astype(bf16).astype(f32)
        tail = jnp.where(hi_row, hi, tail - hi)
        return jnp.concatenate([s[:DH].astype(bf16), tail.astype(bf16)], axis=0)

    def key_state(h):
        f = f_ref[h] * (scale * LOG2E)
        hi = f.astype(bf16)
        split = jnp.concatenate([hi, (f - hi.astype(f32)).astype(bf16)], axis=0)
        fhl[h] = split
        feats = feature_map(k_ref[:, cols(h)], split)
        kf[h] = feats
        flipped = jnp.concatenate([v_ref[:, cols(h)].T, jnp.ones((TAIL, tok), bf16)], axis=0)
        vt[h] = flipped
        s = jnp.dot(flipped, feats, preferred_element_type=f32)
        return jnp.concatenate([s[:DH], jnp.where(hi_row, s[DH:], 0.0)], axis=0)

    def sb_copy(g):
        return remote(sbsend.at[g], sibst.at[g], sb_send.at[g], sb_recv.at[g], sib)

    def x_copy(i):
        return remote(xsend.at[i], xrecv.at[i], x_send.at[i], x_recv.at[i], xn)

    for one in loads[:3]:
        one.wait()

    @pl.loop(0, OWN + 1)
    def _(i):
        @pl.when(i < OWN)
        def _():
            for g in (OWN * (1 - x) + i, OWN * x + i):
                sbsend[g] = key_state(HALF * (1 - c) + g)
                sb_copy(g).start()
                own32[g] = key_state(HALF * c + g)

        @pl.when(i > 0)
        def _():
            g = OWN * (1 - x) + i - 1
            sb_copy(g).wait_recv()
            sb_copy(OWN * x + i - 1).wait_recv()
            xsend[i - 1] = narrow(own32[g] + sibst[g])
            x_copy(i - 1).start()

    w_go(1, z == 0, 0)
    w_go(1, z == 1, 1)
    w_go(2, z == 1, 2)
    w_go(1, z == 2, 1, 2)
    w_go(1, z == 3, 0, 1, 2, 3, 4)
    w_go(2, z == 3, 4, 5)
    for one in own_loads:
        one.start()
    loads[3].wait()
    lower = (lax.broadcasted_iota(jnp.int32, (tok, tok), 1)
             <= lax.broadcasted_iota(jnp.int32, (tok, tok), 0))

    def across(a, b):
        return lax.dot_general(a, b, (((1,), (1,)), ((), ())), preferred_element_type=f32)

    def local_heads(start, stop):
        @pl.loop(start, stop)
        def _(i):
            some = [UNROLL * i + j for j in range(UNROLL)]
            qs = [feature_map(q_ref[:, cols(h)], fhl[h]) for h in some]
            scores = [jnp.where(lower, across(qh, kf[h]), 0.0).astype(bf16)
                      for h, qh in zip(some, qs)]
            sums = [across(s, vt[h]) for h, s in zip(some, scores)]
            for h, qh, total in zip(some, qs, sums):
                qf[h] = qh
                both[h] = total

    steps = heads // UNROLL
    before = jnp.where(z == 0, 0, steps)
    local_heads(0, before)

    at_x0, at_x1 = (x == 0).astype(f32), (x == 1).astype(f32)
    at_c0, at_c1 = (c == 0).astype(f32), (c == 1).astype(f32)

    def sp_copy(g):
        return remote(sbp.at[g], prior.at[HALF * c + g], sp_send.at[g], sp_recv.at[g], sib)

    def put_priors(g, base):
        sbp[g] = base + at_c0 * own32[g]
        sp_copy(g).start()
        prior[HALF * c + g] = base + at_c1 * sibst[g]

    def z_copy(i):
        return remote(back.at[i], below.at[i], z_send.at[i], z_recv.at[i], up)

    def xp_copy(i):
        return remote(xpsend.at[i], xprior.at[i], xp_send.at[i], xp_recv.at[i], xn)

    @pl.loop(0, OWN)
    def _(i):
        g = OWN * x + i
        x_copy(i).wait_recv()

        @pl.when(has_down)
        def _():
            z_copy(i).wait_recv()

        @pl.when(z == 0)
        def _():
            below[i] = jnp.zeros(below.shape[1:], bf16)

        chip = own32[g] + sibst[g]
        under = below[i].astype(f32)
        theirs = xrecv[i].astype(f32)

        @pl.when(has_up)
        def _():
            back[i] = narrow(under + chip + theirs)
            z_copy(i).start()
        xpsend[i] = narrow(under + at_x0 * chip)
        xp_copy(i).start()
        put_priors(g, under + at_x1 * theirs)

    @pl.when(z >= 2)
    def _():
        pl.semaphore_signal(passed, inc=1, device_id=(far, y),
                            device_id_type=pl.DeviceIdType.MESH)

    w_go(1, z == 0, 1, 2, 3, 4, 5)
    w_go(1, z == 1, 2, 3, 4, 5)
    w_go(1, z == 2, 3, 4, 5)
    w_go(1, z == 3, 5)
    w_go(2, z == 3, 6, 7)
    local_heads(before, steps)

    def finish(some):
        done = []
        for h in some:
            p = prior[h]
            hi = p.astype(bf16)
            lo = (p - hi.astype(f32)).astype(bf16)
            old = across(jnp.concatenate([qf[h], qf[h]], axis=1),
                         jnp.concatenate([hi, lo], axis=1))
            here, at = both[h], DH + TAIL // 2
            den = here[:, DH : DH + 1] + old[:, DH : DH + 1] + old[:, at : at + 1]
            done.append(((here[:, :DH] + old[:, :DH]) * (1.0 / den)).astype(bf16))
        for h, part in zip(some, done):
            attb[0, :, cols(h)] = part

    def finish_group(first):
        finish([HALF * c + first + i for i in range(OWN)])

        @pl.loop(first, first + OWN)
        def _(g):
            remote(sbp.at[g], prior.at[HALF * (1 - c) + g], sp_send.at[g], sp_recv.at[g],
                   sib).wait_recv()
        finish([HALF * (1 - c) + first + i for i in range(OWN)])

    finish_group(OWN * x)

    @pl.loop(0, OWN)
    def _(i):
        xp_copy(i).wait_recv()
        put_priors(OWN * (1 - x) + i, xprior[i].astype(f32))

    finish_group(OWN * (1 - x))

    def resume():
        pl.semaphore_wait(passed, 1)

    def att_z(j):
        return remote(attb.at[0, pl.ds(j * ctok, ctok)], attp.at[j, pl.ds(0, ctok)],
                      at_send.at[j], at_recv.at[j], pz)

    def att_fwd(j):
        return remote(attp.at[j, pl.ds(0, ctok)], attp.at[j, pl.ds(ctok, ctok)],
                      at_send.at[CHUNKS + j], at_recv.at[CHUNKS + j], sib)

    att_sib = remote(attb.at[0], attb.at[1], at_send.at[2 * CHUNKS], at_recv.at[2 * CHUNKS], sib)
    att_sib.start()
    pl.when(z == 0)(resume)
    w_go(2, z == 0, 2)
    att_z(0).start()
    w_go(2, z == 0, 3, 4)
    att_z(1).start()
    w_go(2, z == 0, 5)
    att_z(2).start()
    w_go(2, z == 0, 6, 7)
    att_z(3).start()

    keeps_low = y == z // 2
    keeps_high = jnp.logical_not(keeps_low)

    def p_copy(kk, t):
        return pltpu.make_async_remote_copy(
            src_ref=psend.at[kk, t], dst_ref=precv.at[kk, t], send_sem=p_send.at[kk, t],
            recv_sem=p_recv.at[kk, t], device_id=(me, 1 - y), device_id_type=pl.DeviceIdType.MESH)

    def q_copy(kk, j):
        return pltpu.make_async_remote_copy(
            src_ref=qsend.at[kk, j], dst_ref=qrecv.at[kk, j], send_sem=pp_send.at[kk, j],
            recv_sem=pp_recv.at[kk, j], device_id=(me, 1 - y), device_id_type=pl.DeviceIdType.MESH)

    def item(src, hh, t, sums, out, copy):
        piece = jnp.dot(src[t], wbuf[hh], preferred_element_type=f32)
        kk = hh % 4
        keep = (hh // 4 == 0) == keeps_low

        @pl.when(keep)
        def _():
            sums[kk, t] = piece

        @pl.when(jnp.logical_not(keep))
        def _():
            out[kk, t] = piece.astype(bf16)
            copy(kk, t).start()

    def pair(src, slot, t, sums, out, copy):
        weight = jnp.concatenate([wbuf[2 * slot], wbuf[2 * slot + 1]], axis=1)
        piece = jnp.dot(src[t], weight, preferred_element_type=f32)
        first = 2 * (slot % 2)
        keep = (slot // 2 == 0) == keeps_low

        @pl.when(keep)
        def _():
            sums[first, t] = piece[:, :128]
            sums[first + 1, t] = piece[:, 128:]

        @pl.when(jnp.logical_not(keep))
        def _():
            for i in range(2):
                out[first + i, t] = piece[:, 128 * i : 128 * (i + 1)].astype(bf16)
                copy(first + i, t).start()

    def large_pair(slot):
        @pl.loop(0, 2)
        def _(t):
            pair(attb, slot, t, acc, psend, p_copy)

    def small_pair(slot, first_j, many=1):
        @pl.loop(first_j, first_j + many)
        def _(j):
            pair(attp, slot, j, accp, qsend, q_copy)

    def large(first_hh, count, t):
        @pl.loop(first_hh, first_hh + count)
        def _(hh):
            item(attb, hh, t, acc, psend, p_copy)

    def small(first_hh, count, first_j, many=1):
        @pl.loop(0, count * many)
        def _(i):
            item(attp, first_hh + i % count, first_j + i // count, accp, qsend, q_copy)

    def block_of(kk, zz, cc):
        xs = jnp.where(kk // 2 == 0, x, 1 - x)
        return ((zz * 2 + xs) * 2 + cc) * 2 + kk % 2

    def o_copy(kk):
        return remote(osend.at[kk], obuf.at[block_of(kk, z % 2, c)], o_send.at[kk], o_recv.at[kk],
                      sib)

    def op_copy(kk, j, other):
        return remote(opsend.at[kk, j, pl.ds(other * ctok, ctok)],
                      obuf.at[block_of(kk, z % 2, c), pl.ds(j * ctok, ctok)],
                      op_send.at[kk, j, other], op_recv.at[kk, j, other], (pz, pzsib)[other])

    def final_large(cond, first_kk, count):
        @pl.when(cond)
        def _():
            @pl.loop(first_kk, first_kk + count)
            def _(kk):
                p_copy(kk, 1).wait_recv()
                osend[kk] = (acc[kk, 1] + precv[kk, 1].astype(f32)).astype(bf16)
                o_copy(kk).start()
                p_copy(kk, 0).wait_recv()
                obuf[block_of(kk, z % 2, c)] = (acc[kk, 0] + precv[kk, 0].astype(f32)).astype(bf16)

    def final_small(cond, first_kk, count, first_j, many=1):
        @pl.when(cond)
        def _():
            @pl.loop(0, count * many)
            def _(i):
                kk, j = first_kk + i % count, first_j + i // count
                q_copy(kk, j).wait_recv()
                opsend[kk, j] = (accp[kk, j] + qrecv[kk, j].astype(f32)).astype(bf16)
                op_copy(kk, j, 0).start()
                op_copy(kk, j, 1).start()

    def take(j):
        att_z(j).wait_recv()
        att_fwd(j).start()

    def at_planes(cond, takes, forwards):
        @pl.when(cond)
        def _():
            for j in takes:
                take(j)
            forward(*forwards)

    w_go(1, None, 6, 7)
    for one in own_loads:
        one.wait()
    pair(attb, 0, 0, acc, psend, p_copy)
    att_sib.wait_recv()
    pair(attb, 0, 1, acc, psend, p_copy)
    pl.when(z == 1)(resume)
    w_go(2, z == 1, 3, 4, 5, 6, 7)
    at_planes((z == 0) | (z == 1) | (z == 2), (), (4, ))
    forward(0, 1, 2, 3)
    large(4, 1, 0)
    large(4, 1, 1)
    take(0)
    take(1)
    at_planes((z == 3), (), (4, ))
    att_fwd(0).wait_recv()
    att_fwd(1).wait_recv()
    small_pair(0, 0, 2)
    at_planes((z == 1), (), (5, ))
    w_wait(1, 0, 1, 2, 3, 4, 5, 6, 7)
    large_pair(1)
    at_planes((z == 0) | (z == 2), (), (5, ))
    at_planes((z == 2), (), (6, ))
    w_wait(3, 0, 1, 2, 3)
    large(6, 1, 0)
    large(6, 1, 1)
    at_planes((z == 3), (), (5, ))
    small(4, 1, 0, 2)
    at_planes((z == 1), (), (6, 7, ))
    small(6, 1, 0, 2)
    at_planes((z == 0) | (z == 2) | (z == 3), (), (7, ))
    at_planes((z == 0) | (z == 3), (), (6, ))
    large(5, 1, 0)
    large(5, 1, 1)
    small(5, 1, 0, 2)
    small_pair(1, 0, 2)
    take(2)
    take(3)
    att_fwd(2).wait_recv()
    att_fwd(3).wait_recv()
    small_pair(1, 2, 2)
    final_large(keeps_low, 0, 4)
    final_small(keeps_low, 0, 4, 0, 2)
    final_large(keeps_high, 0, 1)
    final_small(keeps_high, 0, 1, 0, 2)
    small(4, 3, 2, 2)
    final_large(keeps_high, 1, 1)
    final_small(keeps_high, 1, 1, 0, 2)
    small_pair(0, 2, 2)
    final_large(keeps_high, 2, 1)
    final_small(keeps_high, 2, 1, 0, 2)
    final_small(keeps_high, 0, 3, 2, 2)
    w_wait(3, 4, 5, 6, 7)
    small(7, 1, 0, 4)
    large(7, 1, 1)
    large(7, 1, 0)
    final_small(keeps_low, 0, 4, 2, 2)
    final_small(keeps_high, 3, 1, 0, 4)
    final_large(keeps_high, 3, 1)

    def show(block):
        shown(block).start()

    def shown(block):
        return pltpu.make_async_copy(
            obuf.at[block], out_ref.at[:, pl.ds(pl.multiple_of(block * 128, 128), 128)],
            show_sem.at[block])

    @pl.loop(0, 4)
    def _(kk):
        show(block_of(kk, z % 2, c))
        o_copy(kk).wait_recv()
        show(block_of(kk, z % 2, 1 - c))
        for other in range(2):
            for j in range(CHUNKS):
                op_copy(kk, j, other).wait_recv()
            show(block_of(kk, 1 - z % 2, c if other == 0 else 1 - c))
        for t in range(2):
            p_copy(kk, t).wait_send()
        o_copy(kk).wait_send()
        for j in range(CHUNKS):
            q_copy(kk, j).wait_send()
            for other in range(2):
                op_copy(kk, j, other).wait_send()

    @pl.loop(0, HALF)
    def _(g):
        sb_copy(g).wait_send()
        sp_copy(g).wait_send()

    @pl.loop(0, OWN)
    def _(i):
        x_copy(i).wait_send()
        xp_copy(i).wait_send()

        @pl.when(has_up)
        def _():
            z_copy(i).wait_send()
    for j in range(CHUNKS):
        att_z(j).wait_send()
        att_fwd(j).wait_send()
    att_sib.wait_send()
    for q in range(WQ):
        for slot in range(1, 4):
            w_out(slot, q).wait_send()

    @pl.loop(0, 16)
    def _(block):
        shown(block).wait()


def fused(queries, keys, values, features, weight):
    tok, columns = queries.shape
    heads = features.shape[0]
    depth = weight.shape[0]
    f32, bf16 = jnp.float32, jnp.bfloat16
    vmem = pltpu.VMEM
    dma = pltpu.SemaphoreType.DMA
    rows = DH + TAIL
    part = tok // CHUNKS
    return pl.pallas_call(
        kernel_body,
        out_shape=jax.ShapeDtypeStruct((tok, columns), bf16),
        in_specs=[pl.BlockSpec(memory_space=pl.ANY)] * 5,
        out_specs=pl.BlockSpec(memory_space=pl.ANY),
        scratch_shapes=[
            vmem((tok, columns), bf16),
            vmem((tok, columns), bf16),
            vmem((tok, columns), bf16),
            vmem(features.shape, f32),
            vmem((8, depth, 128), bf16),
            vmem((heads, 2 * DH, M), bf16),
            vmem((heads, tok, M), bf16),
            vmem((heads, tok, M), bf16),
            vmem((heads, rows, tok), bf16),
            vmem((heads, tok, rows), f32),
            vmem((HALF, rows, M), f32),
            vmem((HALF, rows, M), f32),
            vmem((HALF, rows, M), f32),
            vmem((OWN, rows, M), bf16),
            vmem((OWN, rows, M), bf16),
            vmem((OWN, rows, M), bf16),
            vmem((OWN, rows, M), bf16),
            vmem((OWN, rows, M), bf16),
            vmem((OWN, rows, M), bf16),
            vmem((heads, rows, M), f32),
            vmem((HALF, rows, M), f32),
            vmem((2, tok, columns), bf16),
            vmem((CHUNKS, 2 * part, columns), bf16),
            vmem((4, 2, tok, 128), f32),
            vmem((4, CHUNKS, 2 * part, 128), f32),
            vmem((4, 2, tok, 128), bf16),
            vmem((4, 2, tok, 128), bf16),
            vmem((4, CHUNKS, 2 * part, 128), bf16),
            vmem((4, CHUNKS, 2 * part, 128), bf16),
            vmem((4, tok, 128), bf16),
            vmem((4, CHUNKS, 2 * part, 128), bf16),
            vmem((16, tok, 128), bf16),
            dma((4,)), dma((WQ,)), dma((3, WQ)), dma((3, WQ)), dma((HALF,)), dma((HALF,)),
            dma((OWN,)), dma((OWN,)), dma((OWN,)), dma((OWN,)), dma((OWN,)), dma((OWN,)),
            dma((HALF,)), dma((HALF,)), dma((2 * CHUNKS + 1,)), dma((2 * CHUNKS + 1,)),
            dma((4, 2)), dma((4, 2)), dma((4, CHUNKS)), dma((4, CHUNKS)),
            dma((4,)), dma((4,)), dma((4, CHUNKS, 2)), dma((4, CHUNKS, 2)),
            dma((16,)), pltpu.SemaphoreType.REGULAR,
        ],
        compiler_params=pltpu.CompilerParams(
            collective_id=0, has_side_effects=True, vmem_limit_bytes=60 << 20),
    )(queries, keys, values, features, weight)


def shards(queries, keys, values, features, output_proj_weight):
    fits = (
        lax.axis_size("seq") == PLANE * DEPTH
        and lax.axis_size("head") == 2
        and features.shape == (2 * HALF, DH, M)
        and queries.shape == (256, 2048)
        and output_proj_weight.shape == (2048, 256)
    )
    step = fused if fits else plain
    return step(queries, keys, values, features, output_proj_weight)


def solution(mesh):
    in_specs = (
        P("seq", "head"),
        P("seq", "head"),
        P("seq", "head"),
        P("head", None, None),
        P("head", "seq"),
    )
    return jax.shard_map(
        shards, mesh=mesh, in_specs=in_specs, out_specs=P("seq", "head"), check_vma=False
    )
```

```python
import math

import jax
import jax.numpy as jnp
from jax import lax
from jax.experimental import pallas as pl
from jax.experimental.pallas import tpu as pltpu
from jax.sharding import PartitionSpec as P

DH = 128
M = 256
HIGH = lax.Precision.HIGHEST


def feature_map(x, direction):
    x = x * DH ** (-0.25)
    proj = jnp.einsum("htd,hdm->htm", x, direction, precision=HIGH)
    return jnp.exp(proj - 0.5 * jnp.sum(x * x, axis=-1, keepdims=True)) / math.sqrt(M)


def plain(queries, keys, values, features, output_proj_weight):
    tok_rows = queries.shape[0]
    local_heads = features.shape[0]
    devices, here = lax.axis_size("seq"), lax.axis_index("seq")
    halves, half = lax.axis_size("head"), lax.axis_index("head")

    def split_heads(arr):
        return arr.astype(jnp.float32).reshape(tok_rows, local_heads, DH).transpose(1, 0, 2)

    kf = feature_map(split_heads(keys), features)
    v = split_heads(values)
    v = jnp.concatenate([v, jnp.ones((local_heads, tok_rows, 8), jnp.float32)], axis=2)
    state = jnp.einsum("htp,htk->hpk", v, kf, precision=HIGH)
    states = lax.all_gather(state.astype(jnp.bfloat16), "seq")
    state, weight = lax.optimization_barrier((state, output_proj_weight))
    whole = lax.all_gather(weight, "seq", axis=1, tiled=True)
    qf = feature_map(split_heads(queries), features)
    lower = jnp.tril(jnp.ones((tok_rows, tok_rows), jnp.float32))
    scores = jnp.einsum("htm,hsm->hts", qf, kf, precision=HIGH) * lower
    both = jnp.einsum("hts,hsd->htd", scores, v, precision=HIGH)
    earlier = (jnp.arange(devices) < here)[:, None, None, None]
    prior = jnp.sum(jnp.where(earlier, states.astype(jnp.float32), 0.0), axis=0)
    both = both + jnp.einsum("htk,hpk->htp", qf, prior, precision=HIGH)
    attended = both[:, :, :DH] / both[:, :, DH : DH + 1]
    attended = attended.transpose(1, 0, 2).reshape(tok_rows, local_heads * DH).astype(jnp.bfloat16)
    partial = jnp.dot(attended, whole, preferred_element_type=jnp.float32)
    width = partial.shape[1] // halves
    total = lax.dynamic_slice_in_dim(partial, half * width, width, 1)
    for shift in range(1, halves):
        theirs = lax.rem(half + shift, halves)
        piece = lax.dynamic_slice_in_dim(partial, theirs * width, width, 1).astype(jnp.bfloat16)
        got = lax.ppermute(piece, "head", [(i, (i + shift) % halves) for i in range(halves)])
        total = total + got.astype(jnp.float32)
    return total.astype(jnp.bfloat16)


PLANE, DEPTH = 4, 4
HALF = 8
OWN = 4
TAIL = 16
WQ = 8
CHUNKS = 4
UNROLL = 4
LOG2E = math.log2(math.e)


def kernel_body(q_hbm, k_hbm, v_hbm, f_hbm, w_hbm, out_ref, q_ref, k_ref, v_ref, f_ref, wbuf, fhl,
                kf, qf, vt, both, own32, sibst, sbsend, xsend, xrecv, below, back, xpsend, xprior,
                prior, sbp, attb, attp, acc, accp, psend, precv, qsend, qrecv, osend, opsend, obuf,
                in_sem, w_load, w_send, w_recv, sb_send, sb_recv, x_send, x_recv, z_send, z_recv,
                xp_send, xp_recv, sp_send, sp_recv, at_send, at_recv, p_send, p_recv,
                pp_send, pp_recv, o_send, o_recv, op_send, op_recv, show_sem,
                passed):
    f32, bf16 = jnp.float32, jnp.bfloat16
    tok = q_ref.shape[0]
    ctok = tok // CHUNKS
    heads = f_ref.shape[0]
    qrows = w_hbm.shape[0] // 4
    me, y = lax.axis_index("seq"), lax.axis_index("head")
    z, x, c = me // PLANE, (me // 2) % 2, me % 2
    sib, xn, up, down = me + 1 - 2 * c, me + 2 - 4 * x, me + PLANE, me - PLANE
    pz = me + PLANE - 2 * PLANE * (z % 2)
    pzsib = pz + 1 - 2 * c
    far = me + 2 * PLANE - 4 * PLANE * (z // 2)
    has_up, has_down = z < DEPTH - 1, z > 0

    loads = [pltpu.make_async_copy(a, b, in_sem.at[i]) for i, (a, b) in enumerate(
        ((k_hbm, k_ref), (f_hbm, f_ref), (v_hbm, v_ref), (q_hbm, q_ref)))]
    for one in loads:
        one.start()
    barrier = pltpu.get_barrier_semaphore()

    def greet(device):
        pl.semaphore_signal(barrier, inc=1, device_id=device, device_id_type=pl.DeviceIdType.MESH)

    for device in ((sib, y), (xn, y), (me, 1 - y), (far, y), (pzsib, y)):
        greet(device)

    @pl.when(has_up)
    def _():
        greet((up, y))

    @pl.when(has_down)
    def _():
        greet((down, y))

    pl.semaphore_wait(barrier, 5 + has_up.astype(jnp.int32) + has_down.astype(jnp.int32))

    def remote(src, dst, ssem, rsem, device):
        return pltpu.make_async_remote_copy(
            src_ref=src, dst_ref=dst, send_sem=ssem, recv_sem=rsem, device_id=(device, y),
            device_id_type=pl.DeviceIdType.MESH)

    def place(slot, q):
        return wbuf.at[2 * slot + q // 4, pl.ds((q % 4) * qrows, qrows)]

    def origin(q):
        return w_hbm.at[pl.ds((q % 4) * qrows, qrows), pl.ds((q // 4) * 128, 128)]

    def w_out(slot, q):
        src = origin(q) if slot < 3 else place(2, q)
        return remote(src, place(slot, q), w_send.at[slot - 1, q], w_recv.at[slot - 1, q],
                      far if slot == 2 else xn)

    def w_wait(slot, *qs):
        for q in qs:
            w_out(slot, q).wait_recv()

    def w_go(slot, cond, *qs):
        def start():
            for q in qs:
                w_out(slot, q).start()
        if cond is None:
            start()
        else:
            pl.when(cond)(start)

    def forward(*qs):
        for q in qs:
            w_out(2, q).wait_recv()
            w_out(3, q).start()

    own_loads = [pltpu.make_async_copy(origin(q), place(0, q), w_load.at[q]) for q in range(WQ)]
    w_go(2, z == 0, 0, 1)
    w_go(1, z == 1, 0)
    w_go(2, z == 1, 0, 1)
    w_go(1, z == 2, 0)
    w_go(2, z == 2, 0, 1, 2, 3, 4, 5, 6, 7)
    w_go(2, z == 3, 0, 1, 2, 3)

    scale = DH ** (-0.25)

    def cols(h):
        return pl.ds(pl.multiple_of(h * DH, DH), DH)

    def feature_map(t, split):
        tf = t.astype(f32)
        norm = jnp.sum(tf * tf, axis=-1, keepdims=True) * (0.5 * scale * scale * LOG2E)
        proj = jnp.dot(jnp.concatenate([t, t], axis=1), split, preferred_element_type=f32)
        return jnp.exp2(proj - (norm + 0.5 * math.log2(M))).astype(bf16)

    hi_row = lax.broadcasted_iota(jnp.int32, (TAIL, M), 0) < TAIL // 2

    def narrow(s):
        tail = s[DH:]
        tail = tail + pltpu.roll(tail, TAIL // 2, 0)
        hi = tail.astype(bf16).astype(f32)
        tail = jnp.where(hi_row, hi, tail - hi)
        return jnp.concatenate([s[:DH].astype(bf16), tail.astype(bf16)], axis=0)

    def key_state(h):
        f = f_ref[h] * (scale * LOG2E)
        hi = f.astype(bf16)
        split = jnp.concatenate([hi, (f - hi.astype(f32)).astype(bf16)], axis=0)
        fhl[h] = split
        feats = feature_map(k_ref[:, cols(h)], split)
        kf[h] = feats
        flipped = jnp.concatenate([v_ref[:, cols(h)].T, jnp.ones((TAIL, tok), bf16)], axis=0)
        vt[h] = flipped
        s = jnp.dot(flipped, feats, preferred_element_type=f32)
        return jnp.concatenate([s[:DH], jnp.where(hi_row, s[DH:], 0.0)], axis=0)

    def sb_copy(g):
        return remote(sbsend.at[g], sibst.at[g], sb_send.at[g], sb_recv.at[g], sib)

    def x_copy(i):
        return remote(xsend.at[i], xrecv.at[i], x_send.at[i], x_recv.at[i], xn)

    for one in loads[:3]:
        one.wait()

    @pl.loop(0, OWN + 1)
    def _(i):
        @pl.when(i < OWN)
        def _():
            for g in (OWN * (1 - x) + i, OWN * x + i):
                sbsend[g] = key_state(HALF * (1 - c) + g)
                sb_copy(g).start()
                own32[g] = key_state(HALF * c + g)

        @pl.when(i > 0)
        def _():
            g = OWN * (1 - x) + i - 1
            sb_copy(g).wait_recv()
            sb_copy(OWN * x + i - 1).wait_recv()
            xsend[i - 1] = narrow(own32[g] + sibst[g])
            x_copy(i - 1).start()

    w_go(1, z == 0, 0)
    w_go(1, z == 1, 1)
    w_go(2, z == 1, 2)
    w_go(1, z == 2, 1, 2)
    w_go(1, z == 3, 0, 1, 2, 3, 4)
    w_go(2, z == 3, 4, 5)
    for one in own_loads:
        one.start()
    loads[3].wait()
    lower = (lax.broadcasted_iota(jnp.int32, (tok, tok), 1)
             <= lax.broadcasted_iota(jnp.int32, (tok, tok), 0))

    def across(a, b):
        return lax.dot_general(a, b, (((1,), (1,)), ((), ())), preferred_element_type=f32)

    def local_heads(start, stop):
        @pl.loop(start, stop)
        def _(i):
            some = [UNROLL * i + j for j in range(UNROLL)]
            qs = [feature_map(q_ref[:, cols(h)], fhl[h]) for h in some]
            scores = [jnp.where(lower, across(qh, kf[h]), 0.0).astype(bf16)
                      for h, qh in zip(some, qs)]
            sums = [across(s, vt[h]) for h, s in zip(some, scores)]
            for h, qh, total in zip(some, qs, sums):
                qf[h] = qh
                both[h] = total

    steps = heads // UNROLL
    before = jnp.where(z == 0, 0, steps)
    local_heads(0, before)

    at_x0, at_x1 = (x == 0).astype(f32), (x == 1).astype(f32)
    at_c0, at_c1 = (c == 0).astype(f32), (c == 1).astype(f32)

    def sp_copy(g):
        return remote(sbp.at[g], prior.at[HALF * c + g], sp_send.at[g], sp_recv.at[g], sib)

    def put_priors(g, base):
        sbp[g] = base + at_c0 * own32[g]
        sp_copy(g).start()
        prior[HALF * c + g] = base + at_c1 * sibst[g]

    def z_copy(i):
        return remote(back.at[i], below.at[i], z_send.at[i], z_recv.at[i], up)

    def xp_copy(i):
        return remote(xpsend.at[i], xprior.at[i], xp_send.at[i], xp_recv.at[i], xn)

    @pl.loop(0, OWN)
    def _(i):
        g = OWN * x + i
        x_copy(i).wait_recv()

        @pl.when(has_down)
        def _():
            z_copy(i).wait_recv()

        @pl.when(jnp.logical_and(z >= 2, i == OWN - 1))
        def _():
            pl.semaphore_signal(passed, inc=1, device_id=(far, y),
                                device_id_type=pl.DeviceIdType.MESH)

        @pl.when(z == 0)
        def _():
            below[i] = jnp.zeros(below.shape[1:], bf16)

        chip = own32[g] + sibst[g]
        under = below[i].astype(f32)
        theirs = xrecv[i].astype(f32)

        @pl.when(has_up)
        def _():
            back[i] = narrow(under + chip + theirs)
            z_copy(i).start()
        xpsend[i] = narrow(under + at_x0 * chip)
        xp_copy(i).start()
        put_priors(g, under + at_x1 * theirs)

    w_go(1, z == 0, 1, 2, 3, 4, 5)
    w_go(1, z == 1, 2, 3, 4, 5)
    w_go(1, z == 2, 3, 4, 5)
    w_go(1, z == 3, 5)
    w_go(2, z == 3, 6, 7)
    local_heads(before, steps)

    def finish(some):
        done = []
        for h in some:
            p = prior[h]
            hi = p.astype(bf16)
            lo = (p - hi.astype(f32)).astype(bf16)
            old = across(jnp.concatenate([qf[h], qf[h]], axis=1),
                         jnp.concatenate([hi, lo], axis=1))
            here, at = both[h], DH + TAIL // 2
            den = here[:, DH : DH + 1] + old[:, DH : DH + 1] + old[:, at : at + 1]
            done.append(((here[:, :DH] + old[:, :DH]) * (1.0 / den)).astype(bf16))
        for h, part in zip(some, done):
            attb[0, :, cols(h)] = part

    def finish_group(first):
        finish([HALF * c + first + i for i in range(OWN)])

        @pl.loop(first, first + OWN)
        def _(g):
            remote(sbp.at[g], prior.at[HALF * (1 - c) + g], sp_send.at[g], sp_recv.at[g],
                   sib).wait_recv()
        finish([HALF * (1 - c) + first + i for i in range(OWN)])

    finish_group(OWN * x)

    @pl.loop(0, OWN)
    def _(i):
        xp_copy(i).wait_recv()
        put_priors(OWN * (1 - x) + i, xprior[i].astype(f32))

    finish_group(OWN * (1 - x))

    def resume():
        pl.semaphore_wait(passed, 1)

    def att_z(j):
        return remote(attb.at[0, pl.ds(j * ctok, ctok)], attp.at[j, pl.ds(0, ctok)],
                      at_send.at[j], at_recv.at[j], pz)

    def att_fwd(j):
        return remote(attp.at[j, pl.ds(0, ctok)], attp.at[j, pl.ds(ctok, ctok)],
                      at_send.at[CHUNKS + j], at_recv.at[CHUNKS + j], sib)

    att_sib = remote(attb.at[0], attb.at[1], at_send.at[2 * CHUNKS], at_recv.at[2 * CHUNKS], sib)
    att_sib.start()
    pl.when(z == 0)(resume)
    w_go(2, z == 0, 2)
    att_z(0).start()
    w_go(2, z == 0, 3, 4)
    att_z(1).start()
    w_go(2, z == 0, 5)
    att_z(2).start()
    w_go(2, z == 0, 6, 7)
    att_z(3).start()

    keeps_low = y == z // 2
    keeps_high = jnp.logical_not(keeps_low)

    def p_copy(kk, t):
        return pltpu.make_async_remote_copy(
            src_ref=psend.at[kk, t], dst_ref=precv.at[kk, t], send_sem=p_send.at[kk, t],
            recv_sem=p_recv.at[kk, t], device_id=(me, 1 - y), device_id_type=pl.DeviceIdType.MESH)

    def q_copy(kk, j):
        return pltpu.make_async_remote_copy(
            src_ref=qsend.at[kk, j], dst_ref=qrecv.at[kk, j], send_sem=pp_send.at[kk, j],
            recv_sem=pp_recv.at[kk, j], device_id=(me, 1 - y), device_id_type=pl.DeviceIdType.MESH)

    def item(src, hh, t, sums, out, copy):
        piece = jnp.dot(src[t], wbuf[hh], preferred_element_type=f32)
        kk = hh % 4
        keep = (hh // 4 == 0) == keeps_low

        @pl.when(keep)
        def _():
            sums[kk, t] = piece

        @pl.when(jnp.logical_not(keep))
        def _():
            out[kk, t] = piece.astype(bf16)
            copy(kk, t).start()

    def pair(src, slot, t, sums, out, copy):
        weight = jnp.concatenate([wbuf[2 * slot], wbuf[2 * slot + 1]], axis=1)
        piece = jnp.dot(src[t], weight, preferred_element_type=f32)
        first = 2 * (slot % 2)
        keep = (slot // 2 == 0) == keeps_low

        @pl.when(keep)
        def _():
            sums[first, t] = piece[:, :128]
            sums[first + 1, t] = piece[:, 128:]

        @pl.when(jnp.logical_not(keep))
        def _():
            for i in range(2):
                out[first + i, t] = piece[:, 128 * i : 128 * (i + 1)].astype(bf16)
                copy(first + i, t).start()

    def large_pair(slot):
        @pl.loop(0, 2)
        def _(t):
            pair(attb, slot, t, acc, psend, p_copy)

    def small_pair(slot, first_j, many=1):
        @pl.loop(first_j, first_j + many)
        def _(j):
            pair(attp, slot, j, accp, qsend, q_copy)

    def large(first_hh, count, t):
        @pl.loop(first_hh, first_hh + count)
        def _(hh):
            item(attb, hh, t, acc, psend, p_copy)

    def small(first_hh, count, first_j, many=1):
        @pl.loop(0, count * many)
        def _(i):
            item(attp, first_hh + i % count, first_j + i // count, accp, qsend, q_copy)

    def block_of(kk, zz, cc):
        xs = jnp.where(kk // 2 == 0, x, 1 - x)
        return ((zz * 2 + xs) * 2 + cc) * 2 + kk % 2

    def o_copy(kk):
        return remote(osend.at[kk], obuf.at[block_of(kk, z % 2, c)], o_send.at[kk], o_recv.at[kk],
                      sib)

    def op_copy(kk, j, other):
        return remote(opsend.at[kk, j, pl.ds(other * ctok, ctok)],
                      obuf.at[block_of(kk, z % 2, c), pl.ds(j * ctok, ctok)],
                      op_send.at[kk, j, other], op_recv.at[kk, j, other], (pz, pzsib)[other])

    def final_large(cond, first_kk, count):
        @pl.when(cond)
        def _():
            @pl.loop(first_kk, first_kk + count)
            def _(kk):
                p_copy(kk, 1).wait_recv()
                osend[kk] = (acc[kk, 1] + precv[kk, 1].astype(f32)).astype(bf16)
                o_copy(kk).start()
                p_copy(kk, 0).wait_recv()
                obuf[block_of(kk, z % 2, c)] = (acc[kk, 0] + precv[kk, 0].astype(f32)).astype(bf16)

    def final_small(cond, first_kk, count, first_j, many=1):
        @pl.when(cond)
        def _():
            @pl.loop(0, count * many)
            def _(i):
                kk, j = first_kk + i % count, first_j + i // count
                q_copy(kk, j).wait_recv()
                opsend[kk, j] = (accp[kk, j] + qrecv[kk, j].astype(f32)).astype(bf16)
                op_copy(kk, j, 0).start()
                op_copy(kk, j, 1).start()

    def take(j):
        att_z(j).wait_recv()
        att_fwd(j).start()

    def at_planes(cond, takes, forwards):
        @pl.when(cond)
        def _():
            for j in takes:
                take(j)
            forward(*forwards)

    w_go(1, None, 6, 7)
    for one in own_loads:
        one.wait()
    pair(attb, 0, 0, acc, psend, p_copy)
    att_sib.wait_recv()
    pair(attb, 0, 1, acc, psend, p_copy)
    pl.when(z == 1)(resume)
    w_go(2, z == 1, 3, 4, 5, 6, 7)
    at_planes((z == 0) | (z == 1) | (z == 2), (), (4, ))
    forward(0, 1, 2, 3)
    large(4, 1, 0)
    large(4, 1, 1)
    take(0)
    take(1)
    at_planes((z == 3), (), (4, ))
    att_fwd(0).wait_recv()
    att_fwd(1).wait_recv()
    small_pair(0, 0, 2)
    at_planes((z == 1), (), (5, ))
    w_wait(1, 0, 1, 2, 3, 4, 5, 6, 7)
    large_pair(1)
    at_planes((z == 0) | (z == 2), (), (5, ))
    at_planes((z == 2), (), (6, ))
    w_wait(3, 0, 1, 2, 3)
    large(6, 1, 0)
    large(6, 1, 1)
    at_planes((z == 3), (), (5, ))
    small(4, 1, 0, 2)
    at_planes((z == 1), (), (6, 7, ))
    small(6, 1, 0, 2)
    at_planes((z == 0) | (z == 2) | (z == 3), (), (7, ))
    at_planes((z == 0) | (z == 3), (), (6, ))
    large(5, 1, 0)
    large(5, 1, 1)
    small(5, 1, 0, 2)
    small_pair(1, 0, 2)
    take(2)
    take(3)
    att_fwd(2).wait_recv()
    att_fwd(3).wait_recv()
    small_pair(1, 2, 2)
    final_large(keeps_low, 0, 4)
    final_small(keeps_low, 0, 4, 0, 2)
    final_large(keeps_high, 0, 1)
    final_small(keeps_high, 0, 1, 0, 2)
    small(4, 3, 2, 2)
    final_large(keeps_high, 1, 1)
    final_small(keeps_high, 1, 1, 0, 2)
    small_pair(0, 2, 2)
    final_large(keeps_high, 2, 1)
    final_small(keeps_high, 2, 1, 0, 2)
    final_small(keeps_high, 0, 3, 2, 2)
    w_wait(3, 4, 5, 6, 7)
    small(7, 1, 0, 4)
    large(7, 1, 1)
    large(7, 1, 0)
    final_small(keeps_low, 0, 4, 2, 2)
    final_small(keeps_high, 3, 1, 0, 4)
    final_large(keeps_high, 3, 1)

    def show(block):
        shown(block).start()

    def shown(block):
        return pltpu.make_async_copy(
            obuf.at[block], out_ref.at[:, pl.ds(pl.multiple_of(block * 128, 128), 128)],
            show_sem.at[block])

    @pl.loop(0, 4)
    def _(kk):
        show(block_of(kk, z % 2, c))
        o_copy(kk).wait_recv()
        show(block_of(kk, z % 2, 1 - c))
        for other in range(2):
            for j in range(CHUNKS):
                op_copy(kk, j, other).wait_recv()
            show(block_of(kk, 1 - z % 2, c if other == 0 else 1 - c))
        for t in range(2):
            p_copy(kk, t).wait_send()
        o_copy(kk).wait_send()
        for j in range(CHUNKS):
            q_copy(kk, j).wait_send()
            for other in range(2):
                op_copy(kk, j, other).wait_send()

    @pl.loop(0, HALF)
    def _(g):
        sb_copy(g).wait_send()
        sp_copy(g).wait_send()

    @pl.loop(0, OWN)
    def _(i):
        x_copy(i).wait_send()
        xp_copy(i).wait_send()

        @pl.when(has_up)
        def _():
            z_copy(i).wait_send()
    for j in range(CHUNKS):
        att_z(j).wait_send()
        att_fwd(j).wait_send()
    att_sib.wait_send()
    for q in range(WQ):
        for slot in range(1, 4):
            w_out(slot, q).wait_send()

    @pl.loop(0, 16)
    def _(block):
        shown(block).wait()


def fused(queries, keys, values, features, weight):
    tok, columns = queries.shape
    heads = features.shape[0]
    depth = weight.shape[0]
    f32, bf16 = jnp.float32, jnp.bfloat16
    vmem = pltpu.VMEM
    dma = pltpu.SemaphoreType.DMA
    rows = DH + TAIL
    part = tok // CHUNKS
    return pl.pallas_call(
        kernel_body,
        out_shape=jax.ShapeDtypeStruct((tok, columns), bf16),
        in_specs=[pl.BlockSpec(memory_space=pl.ANY)] * 5,
        out_specs=pl.BlockSpec(memory_space=pl.ANY),
        scratch_shapes=[
            vmem((tok, columns), bf16),
            vmem((tok, columns), bf16),
            vmem((tok, columns), bf16),
            vmem(features.shape, f32),
            vmem((8, depth, 128), bf16),
            vmem((heads, 2 * DH, M), bf16),
            vmem((heads, tok, M), bf16),
            vmem((heads, tok, M), bf16),
            vmem((heads, rows, tok), bf16),
            vmem((heads, tok, rows), f32),
            vmem((HALF, rows, M), f32),
            vmem((HALF, rows, M), f32),
            vmem((HALF, rows, M), f32),
            vmem((OWN, rows, M), bf16),
            vmem((OWN, rows, M), bf16),
            vmem((OWN, rows, M), bf16),
            vmem((OWN, rows, M), bf16),
            vmem((OWN, rows, M), bf16),
            vmem((OWN, rows, M), bf16),
            vmem((heads, rows, M), f32),
            vmem((HALF, rows, M), f32),
            vmem((2, tok, columns), bf16),
            vmem((CHUNKS, 2 * part, columns), bf16),
            vmem((4, 2, tok, 128), f32),
            vmem((4, CHUNKS, 2 * part, 128), f32),
            vmem((4, 2, tok, 128), bf16),
            vmem((4, 2, tok, 128), bf16),
            vmem((4, CHUNKS, 2 * part, 128), bf16),
            vmem((4, CHUNKS, 2 * part, 128), bf16),
            vmem((4, tok, 128), bf16),
            vmem((4, CHUNKS, 2 * part, 128), bf16),
            vmem((16, tok, 128), bf16),
            dma((4,)), dma((WQ,)), dma((3, WQ)), dma((3, WQ)), dma((HALF,)), dma((HALF,)),
            dma((OWN,)), dma((OWN,)), dma((OWN,)), dma((OWN,)), dma((OWN,)), dma((OWN,)),
            dma((HALF,)), dma((HALF,)), dma((2 * CHUNKS + 1,)), dma((2 * CHUNKS + 1,)),
            dma((4, 2)), dma((4, 2)), dma((4, CHUNKS)), dma((4, CHUNKS)),
            dma((4,)), dma((4,)), dma((4, CHUNKS, 2)), dma((4, CHUNKS, 2)),
            dma((16,)), pltpu.SemaphoreType.REGULAR,
        ],
        compiler_params=pltpu.CompilerParams(
            collective_id=0, has_side_effects=True, vmem_limit_bytes=60 << 20),
    )(queries, keys, values, features, weight)


def shards(queries, keys, values, features, output_proj_weight):
    fits = (
        lax.axis_size("seq") == PLANE * DEPTH
        and lax.axis_size("head") == 2
        and features.shape == (2 * HALF, DH, M)
        and queries.shape == (256, 2048)
        and output_proj_weight.shape == (2048, 256)
    )
    step = fused if fits else plain
    return step(queries, keys, values, features, output_proj_weight)


def solution(mesh):
    in_specs = (
        P("seq", "head"),
        P("seq", "head"),
        P("seq", "head"),
        P("head", None, None),
        P("head", "seq"),
    )
    return jax.shard_map(
        shards, mesh=mesh, in_specs=in_specs, out_specs=P("seq", "head"), check_vma=False
    )
```
